32 devices in a mesh: seq: 16 (over z, x, core), ch: 2 (over y).
Axes of the slice: x: 2, y: 2, z: 4, core: 2. Of those that a mesh axis runs over, the one named last changes fastest.
Arguments:
- tokens: bfloat16 [131072, 1024], P('seq', 'ch'), may hold values from -6 to 6
- right_block: bfloat16 [1024, 1024], P('seq'), may hold values from -0.1875 to 0.1875
- twiddle: bfloat16 [128, 1024], P('seq'), may hold values from -4 to 4
- left_block: bfloat16 [128, 128], replicated, may hold values from -0.5 to 0.5
- gain: float32 [1024], replicated, may hold values from 0.1 to 1.9
- mix_weight: bfloat16 [4, 256, 256], replicated, may hold values from -0.375 to 0.375
Outputs:
- layer_out: bfloat16 [131072, 1024], P(('seq', 'ch'))
The draws below stay inside these ranges and needn't reach their ends.
All inputs are finite; a program needn't handle non-finite values.
Results may differ from the reference program's by a relative error of at most 0.007.
Values may be sent and summed in bfloat16 or wider, within the bound.
No kernel may reach another device: no remote copies, remote signals or barrier semaphores. Data moves between devices by JAX's collectives and lax.ppermute only.
A program may use at most 128 MiB of HBM per device.

```python
import jax
import jax.numpy as jnp
from jax import lax

D = 1024
BS = 1024
CBLK = 256
NB = 128
TOKENS = 131072
N_CH = 2


def shard_levels(own_key, extent, split, low, top_value):
    level = 1.0
    for dim, blocks in split:
        draws = jax.random.uniform(jax.random.fold_in(jax.random.fold_in(own_key, 6), dim), (blocks,), jnp.float32, low / len(split), top_value / len(split))
        level = level * jnp.repeat(jnp.exp(draws), extent[dim] // blocks).reshape((-1,) + (1,) * (len(extent) - 1 - dim))
    return level


def scatter_about(key, dims, scale, most, cuts=(), held_as=jnp.bfloat16):
    level = shard_levels(key, dims, cuts, -0.22, 0.18) if cuts else 1.0
    entries = jax.random.normal(key, dims, jnp.float32) * scale * level
    return jnp.minimum(jnp.maximum(entries, -most), most).astype(held_as)


def setup_inputs(seed: int = 0) -> dict:
    keys = jax.random.split(jax.random.key(seed), 7)
    tokens = scatter_about(keys[0], (TOKENS, D), 1.0, 6.0, ((0, 16), (1, 2)))
    right_block = scatter_about(keys[1], (BS, BS), BS ** -0.5, 0.1875, ((0, 16),))
    twiddle = scatter_about(keys[2], (NB, BS), 1.0, 4.0, ((0, 16),))
    left_block = scatter_about(keys[3], (NB, NB), NB ** -0.5, 0.5)
    gain = jnp.clip(1.0 + 0.18 * jax.random.normal(keys[4], (D,), jnp.float32), 0.1, 1.9)
    mix_weight = scatter_about(keys[5], (D // CBLK, CBLK, CBLK), CBLK ** -0.5, 0.375)
    return {"tokens": tokens, "right_block": right_block, "twiddle": twiddle, "left_block": left_block, "gain": gain, "mix_weight": mix_weight}


def reference(tokens, right_block, twiddle, left_block, gain, mix_weight):
    group_size = D // N_CH
    channel_groups = tokens.reshape(NB, BS, N_CH, group_size).transpose(2, 0, 1, 3)
    right_f32 = right_block.astype(jnp.float32)
    left_f32 = left_block.astype(jnp.float32)
    twiddle_f32 = twiddle.astype(jnp.float32)[:, :, None]

    def mix_sequence(channel_block):
        section_one = jnp.einsum('abc,bk->akc', channel_block.astype(jnp.float32), right_f32) * twiddle_f32
        rounded = lax.optimization_barrier(section_one.astype(jnp.bfloat16)).astype(jnp.float32)
        return jnp.einsum('ij,jbc->ibc', left_f32, rounded).astype(jnp.bfloat16)
    sequence_mixed = lax.map(mix_sequence, channel_groups)
    sequence_mixed = sequence_mixed.transpose(1, 2, 0, 3).reshape(NB, BS, D)
    input_rows = tokens.reshape(NB, BS, D)
    weight_f32 = mix_weight.astype(jnp.float32)

    def mix_channels(row_pair):
        seq_part, input_part = row_pair
        gated = (seq_part.astype(jnp.float32) * jax.nn.silu(input_part.astype(jnp.float32))).astype(jnp.bfloat16)
        values = lax.optimization_barrier(gated).astype(jnp.float32)
        inverse_rms = lax.rsqrt(lax.optimization_barrier(jnp.mean(values * values, axis=-1, keepdims=True)) + 1e-05)
        normed = (values * inverse_rms * gain).astype(jnp.bfloat16)
        normed = lax.optimization_barrier(normed).astype(jnp.float32).reshape(BS, D // CBLK, CBLK)
        result = jnp.einsum('tki,kij->tkj', normed, weight_f32)
        return result.astype(jnp.bfloat16).reshape(BS, D)
    layer_out = lax.map(mix_channels, (sequence_mixed, input_rows))
    return layer_out.reshape(NB * BS, D)
```

```python
import functools

import jax
import jax.numpy as jnp
from jax import lax
from jax.experimental import pallas as pl
from jax.experimental.pallas import tpu as pltpu
from jax.sharding import PartitionSpec as P

ANY = pl.BlockSpec(memory_space=pl.ANY)
VMEM = pl.BlockSpec(memory_space=pltpu.VMEM)
LANES = 256
CHUNKS = 2


def other(index, mask):
    return jnp.bitwise_xor(index, mask)


def gather_order(count):
    masks = [0]
    bit = count // 2
    while bit:
        masks = masks + [m ^ bit for m in masks]
        bit //= 2
    return masks


class Plan:
    def __init__(self, tokens, right_block, twiddle, left_block, mix_weight):
        self.seq = lax.axis_size("seq")
        self.ch = lax.axis_size("ch")
        self.width = right_block.shape[1]
        self.rows = tokens.shape[0] // self.width
        self.local = tokens.shape[1]
        self.right_rows = right_block.shape[0]
        self.all_rows = left_block.shape[0]
        self.chunk = self.local // CHUNKS
        self.own = self.chunk // self.seq
        self.out_rows = self.rows // self.ch
        self.channels = self.local * self.ch
        self.mix = mix_weight.shape[1]
        pad = self.right_rows + twiddle.shape[0]
        self.gather_rows = pad + (-pad) % 16

    def fits(self):
        s, c = self.seq, self.ch
        return (
            s > 1
            and s <= 16
            and c <= 4
            and s & (s - 1) == 0
            and c & (c - 1) == 0
            and self.own % 16 == 0
            and self.own > 0
            and self.chunk % 128 == 0
            and self.rows % 8 == 0
            and 16 % self.rows == 0
            and self.rows % c == 0
            and self.all_rows % 16 == 0
            and self.right_rows % 16 == 0
            and self.width % LANES == 0
            and self.mix % 128 == 0
        )


def prep_kernel(plan, x_ref, *rest):
    s, c = plan.seq, plan.ch
    pieces, shares = rest[:s], rest[s : s + c]
    turned, piece_sem, share_sem = rest[s + c :]
    me, y = lax.axis_index("seq"), lax.axis_index("ch")
    a = pl.program_id(0)
    turned[a] = x_ref[...].T

    def rows_of(m):
        return pl.ds(pl.multiple_of(other(me, m) * plan.own, plan.own), plan.own)

    for m in range(s):
        pltpu.make_async_copy(
            turned.at[a, rows_of(m), :], pieces[m].at[a], piece_sem.at[m]
        ).start()

    @pl.when(a == plan.rows - 1)
    def _():
        copies = [
            pltpu.make_async_copy(
                turned.at[pl.ds(other(y, m) * plan.out_rows, plan.out_rows)],
                shares[m],
                share_sem.at[m],
            )
            for m in range(c)
        ]
        for copy in copies:
            copy.start()
        for m in range(s):
            pltpu.make_async_copy(turned.at[:, rows_of(m), :], pieces[m], piece_sem.at[m]).wait()
        for copy in copies:
            copy.wait()


def prep(plan, tokens, chunk):
    shapes = [jax.ShapeDtypeStruct((plan.rows, plan.own, plan.width), jnp.bfloat16)] * plan.seq
    shapes += [
        jax.ShapeDtypeStruct((plan.out_rows, plan.chunk, plan.width), jnp.bfloat16)
    ] * plan.ch
    out = pl.pallas_call(
        functools.partial(prep_kernel, plan),
        out_shape=shapes,
        grid=(plan.rows,),
        in_specs=[pl.BlockSpec((plan.width, plan.chunk), lambda a: (a, chunk))],
        out_specs=[ANY] * len(shapes),
        scratch_shapes=[
            pltpu.VMEM((plan.rows, plan.chunk, plan.width), jnp.bfloat16),
            pltpu.SemaphoreType.DMA((plan.seq,)),
            pltpu.SemaphoreType.DMA((plan.ch,)),
        ],
        cost_estimate=pl.CostEstimate(
            flops=0,
            bytes_accessed=5 * plan.rows * plan.chunk * plan.width,
            transcendentals=0,
        ),
        name="prep",
    )(tokens)
    return out[: plan.seq], out[plan.seq :]


def sections_kernel(plan, *refs):
    s, c, own = plan.seq, plan.ch, plan.own
    pieces, gathered, left = refs[:s], refs[s : s + 2], refs[s + 2]
    outs = refs[s + 3 : s + 3 + s * c]
    x, right, twiddle, first, mixed, done, sem_x, sem_r, sem_t, sem_o = refs[s + 3 + s * c :]
    me, y = lax.axis_index("seq"), lax.axis_index("ch")
    copies = []
    for j, m in enumerate(gather_order(s)):
        source = gathered[j // (s // 2)].at[j % (s // 2)]
        who = other(me, m)
        at = pl.ds(pl.multiple_of(who * plan.right_rows, plan.right_rows), plan.right_rows)
        copies.append(
            pltpu.make_async_copy(source.at[pl.ds(0, plan.right_rows)], right.at[at], sem_r.at[j])
        )
        copies.append(
            pltpu.make_async_copy(
                source.at[pl.ds(plan.right_rows, plan.rows)], twiddle.at[who], sem_t.at[j]
            )
        )
    for m in range(s):
        at = pl.ds(other(me, m) * plan.rows, plan.rows)
        copies.append(pltpu.make_async_copy(pieces[m], x.at[at], sem_x.at[m]))
    for copy in copies:
        copy.start()
    for copy in copies:
        copy.wait()
    step = 16

    def tile(kt, carry):
        ks = pl.ds(pl.multiple_of(kt * LANES, LANES), LANES)

        def section_one(t, carry):
            rows = x[pl.ds(t * step, step)].reshape(step * own, plan.width)
            value = jnp.dot(rows, right[:, ks], preferred_element_type=jnp.float32)
            value = value.reshape(step, own, LANES)
            group = step // plan.rows
            factor = twiddle[pl.ds(t * group, group), :, ks].astype(jnp.float32)
            value = value * factor.reshape(step, LANES)[:, None, :]
            at = pl.ds(pl.multiple_of(t * step, step), step)
            first[:, at, :] = jnp.swapaxes(value, 0, 1).astype(jnp.bfloat16)
            return carry

        lax.fori_loop(0, plan.all_rows // step, section_one, 0)
        for q in range(own):
            mixed[q] = jnp.dot(left[...], first[q], preferred_element_type=jnp.float32)

        def turn(t, carry):
            at = pl.ds(pl.multiple_of(t * step, step), step)
            value = jnp.swapaxes(mixed[:, at, :], 0, 1)
            done[pl.ds(t * step, step), :, ks] = value.astype(jnp.bfloat16)
            return carry

        lax.fori_loop(0, plan.all_rows // step, turn, 0)
        return carry

    lax.fori_loop(0, plan.width // LANES, tile, 0)
    copies = []
    for m in range(s):
        for n in range(c):
            at = other(me, m) * plan.rows + other(y, n) * plan.out_rows
            copies.append(
                pltpu.make_async_copy(
                    done.at[pl.ds(at, plan.out_rows)], outs[m * c + n], sem_o.at[m * c + n]
                )
            )
    for copy in copies:
        copy.start()
    for copy in copies:
        copy.wait()


def sections(plan, pieces, gathered, left):
    s, c, own, width, bf16 = plan.seq, plan.ch, plan.own, plan.width, jnp.bfloat16
    shapes = [jax.ShapeDtypeStruct((plan.out_rows, own, width), bf16)] * (s * c)
    flops = 2 * plan.all_rows * own * width * (width + plan.all_rows)
    return pl.pallas_call(
        functools.partial(sections_kernel, plan),
        out_shape=shapes,
        in_specs=[ANY] * (s + 2) + [VMEM],
        out_specs=[ANY] * len(shapes),
        scratch_shapes=[
            pltpu.VMEM((plan.all_rows, own, width), bf16),
            pltpu.VMEM((s * plan.right_rows, width), bf16),
            pltpu.VMEM((s, plan.rows, width), bf16),
            pltpu.VMEM((own, plan.all_rows, LANES), bf16),
            pltpu.VMEM((own, plan.all_rows, LANES), jnp.float32),
            pltpu.VMEM((plan.all_rows, own, width), bf16),
            pltpu.SemaphoreType.DMA((s,)),
            pltpu.SemaphoreType.DMA((s,)),
            pltpu.SemaphoreType.DMA((s,)),
            pltpu.SemaphoreType.DMA((s * c,)),
        ],
        cost_estimate=pl.CostEstimate(
            flops=flops,
            bytes_accessed=4 * plan.all_rows * own * width + 2 * width * width,
            transcendentals=0,
        ),
        name="sections",
    )(*pieces, *gathered, left)


def final_kernel(plan, *refs):
    s, c = plan.seq, plan.ch
    count = CHUNKS * s * c
    pieces, shares = refs[:count], refs[count : count + CHUNKS * c]
    gain, weight, out, mixed, inputs, sem_m, sem_i = refs[count + CHUNKS * c :]
    me, y = lax.axis_index("seq"), lax.axis_index("ch")
    i = pl.program_id(0)

    @pl.when(i == 0)
    def _():
        for r in range(plan.out_rows):
            for k in range(CHUNKS):
                for n in range(c):
                    base = other(y, n) * plan.local + k * plan.chunk
                    at = pl.ds(pl.multiple_of(base, plan.chunk), plan.chunk)
                    pltpu.make_async_copy(
                        shares[k * c + n].at[r], inputs.at[r, at], sem_i.at[r]
                    ).start()
                    for m in range(s):
                        row = pl.multiple_of(base + other(me, m) * plan.own, plan.own)
                        pltpu.make_async_copy(
                            pieces[(k * s + m) * c + n].at[r],
                            mixed.at[r, pl.ds(row, plan.own)],
                            sem_m.at[r],
                        ).start()

    pltpu.make_async_copy(inputs.at[i], inputs.at[i], sem_i.at[i]).wait()
    pltpu.make_async_copy(mixed.at[i], mixed.at[i], sem_m.at[i]).wait()
    blocks = plan.channels // plan.mix

    def tile(kt, carry):
        ks = pl.ds(pl.multiple_of(kt * LANES, LANES), LANES)
        total = jnp.zeros((1, LANES), jnp.float32)
        for j in range(blocks):
            rs = pl.ds(j * plan.mix, plan.mix)
            value = mixed[i, rs, ks].astype(jnp.float32)
            gate = inputs[i, rs, ks].astype(jnp.float32)
            gated = (value * (gate / (1.0 + jnp.exp(-gate)))).astype(jnp.bfloat16)
            mixed[i, rs, ks] = gated
            gated = gated.astype(jnp.float32)
            total = total + jnp.sum(gated * gated, axis=0, keepdims=True)
        inverse = lax.rsqrt(total * (1.0 / plan.channels) + 1e-05)
        for j in range(blocks):
            rs = pl.ds(j * plan.mix, plan.mix)
            normed = (mixed[i, rs, ks].astype(jnp.float32) * inverse * gain[rs, :]).astype(
                jnp.bfloat16
            )
            result = lax.dot_general(
                normed,
                weight[j],
                (((0,), (0,)), ((), ())),
                preferred_element_type=jnp.float32,
            )
            out[ks, rs] = result.astype(jnp.bfloat16)
        return carry

    lax.fori_loop(0, plan.width // LANES, tile, 0)


def final(plan, pieces, shares, gain, weight):
    bf16 = jnp.bfloat16
    size = plan.out_rows * plan.width
    return pl.pallas_call(
        functools.partial(final_kernel, plan),
        out_shape=jax.ShapeDtypeStruct((size, plan.channels), bf16),
        grid=(plan.out_rows,),
        in_specs=[ANY] * (len(pieces) + len(shares)) + [VMEM, VMEM],
        out_specs=pl.BlockSpec((plan.width, plan.channels), lambda i: (i, 0)),
        scratch_shapes=[
            pltpu.VMEM((plan.out_rows, plan.channels, plan.width), bf16),
            pltpu.VMEM((plan.out_rows, plan.channels, plan.width), bf16),
            pltpu.SemaphoreType.DMA((plan.out_rows,)),
            pltpu.SemaphoreType.DMA((plan.out_rows,)),
        ],
        cost_estimate=pl.CostEstimate(
            flops=2 * size * plan.channels * plan.mix,
            bytes_accessed=6 * size * plan.channels,
            transcendentals=size * plan.channels,
        ),
        name="final",
    )(*pieces, *shares, jnp.broadcast_to(gain[:, None], (plan.channels, LANES)), weight)


def swap(value, seq_mask, ch_mask, s, c):
    if seq_mask == 0 and ch_mask == 0:
        return value
    pairs = [
        (i * c + j, (i ^ seq_mask) * c + (j ^ ch_mask)) for i in range(s) for j in range(c)
    ]
    return lax.ppermute(value, ("seq", "ch"), pairs)


def gather(plan, right_block, twiddle):
    s = plan.seq
    pad = plan.gather_rows - right_block.shape[0] - twiddle.shape[0]
    held = jnp.concatenate(
        [right_block, twiddle, jnp.zeros((pad, plan.width), jnp.bfloat16)], axis=0
    )[None]
    bit = s // 2
    while bit:
        got = swap(held, bit, 0, s, plan.ch)
        if bit > 1:
            held = jnp.concatenate([held, got], axis=0)
        bit //= 2
    return held, got


def permuted_body(plan, tokens, right_block, twiddle, left_block, gain, mix_weight):
    s, c = plan.seq, plan.ch
    gathered = gather(plan, right_block, twiddle)
    arrived, shares = [], []
    for k in range(CHUNKS):
        pieces, share = prep(plan, tokens, k)
        arrived.append([swap(pieces[m], m, 0, s, c) for m in range(s)])
        shares += [swap(share[n], 0, n, s, c) for n in range(c)]
    landed = []
    for k in range(CHUNKS):
        outs = sections(plan, arrived[k], gathered, left_block)
        landed += [swap(outs[m * c + n], m, n, s, c) for m in range(s) for n in range(c)]
    return final(plan, landed, shares, gain, mix_weight)


def plain_body(tokens, right_block, twiddle, left_block, gain, mix_weight):
    row_width = right_block.shape[1]
    row_count = tokens.shape[0] // row_width
    local_width = tokens.shape[1]
    inputs = tokens.reshape(row_count, row_width, local_width)
    whole_right = lax.all_gather(right_block, "seq", axis=0, tiled=True)
    first_section = jnp.einsum(
        "abc,bk->akc", inputs, whole_right, preferred_element_type=jnp.float32
    )
    spread = (first_section * twiddle.astype(jnp.float32)[:, :, None]).astype(jnp.bfloat16)
    mixed_rows = jnp.einsum(
        "ij,jbc->ibc",
        left_block,
        lax.all_to_all(spread, "seq", split_axis=1, concat_axis=0, tiled=True),
        preferred_element_type=jnp.float32,
    ).astype(jnp.bfloat16)
    sequence_mixed = lax.all_to_all(mixed_rows, "seq", split_axis=0, concat_axis=1, tiled=True)
    gated = (sequence_mixed.astype(jnp.float32) * jax.nn.silu(inputs.astype(jnp.float32))).astype(
        jnp.bfloat16
    )
    ch_count = lax.axis_size("ch")
    pieces = gated.reshape(ch_count, row_count * row_width // ch_count, local_width)
    shard_piece = lax.all_to_all(pieces, "ch", split_axis=0, concat_axis=2, tiled=True)
    values = shard_piece.astype(jnp.float32)
    inverse_rms = lax.rsqrt(jnp.mean(values * values, axis=-1, keepdims=True) + 1e-05)
    normed = (values * inverse_rms * gain).astype(jnp.bfloat16)
    block_count = mix_weight.shape[0]
    block_width = mix_weight.shape[1]
    normed = normed.reshape(shard_piece.shape[0], shard_piece.shape[1], block_count, block_width)
    result = jnp.einsum("otki,kij->otkj", normed, mix_weight, preferred_element_type=jnp.float32)
    mixed_out = result.astype(jnp.bfloat16).reshape(shard_piece.shape)
    return mixed_out.reshape(mixed_out.shape[1], mixed_out.shape[2])


def body(tokens, right_block, twiddle, left_block, gain, mix_weight):
    plan = Plan(tokens, right_block, twiddle, left_block, mix_weight)
    if plan.fits():
        return permuted_body(plan, tokens, right_block, twiddle, left_block, gain, mix_weight)
    return plain_body(tokens, right_block, twiddle, left_block, gain, mix_weight)


def solution(mesh):
    in_specs = (P("seq", "ch"), P("seq", None), P("seq", None), P(), P(), P())
    out_specs = P(("seq", "ch"), None)
    return jax.shard_map(body, mesh=mesh, in_specs=in_specs, out_specs=out_specs, check_vma=False)
```

```python
import functools

import jax
import jax.numpy as jnp
from jax import lax
from jax.experimental import pallas as pl
from jax.experimental.pallas import tpu as pltpu
from jax.sharding import PartitionSpec as P


ANY = pl.BlockSpec(memory_space=pl.ANY)
VMEM = pl.BlockSpec(memory_space=pltpu.VMEM)
LANES = 256
CHUNKS = 2
STEP = 16


class Plan:
    def __init__(self, tokens, right_block, twiddle, left_block, mix_weight):
        self.seq = lax.axis_size("seq")
        self.ch = lax.axis_size("ch")
        self.width = right_block.shape[1]
        self.rows = tokens.shape[0] // self.width
        self.local = tokens.shape[1]
        self.right_rows = right_block.shape[0]
        self.all_rows = left_block.shape[0]
        self.chunk = self.local // CHUNKS
        self.own = self.chunk // self.seq
        self.out_rows = self.rows // self.ch
        self.channels = self.local * self.ch
        self.mix = mix_weight.shape[1]
        self.near = 1
        while self.near * self.near < self.seq:
            self.near *= 2
        pad = self.right_rows + twiddle.shape[0]
        self.gather_rows = pad + (-pad) % 16

    def fits(self):
        s, c = self.seq, self.ch
        return (
            s > 1
            and s <= 16
            and c > 1
            and c <= 4
            and s & (s - 1) == 0
            and c & (c - 1) == 0
            and self.own % 16 == 0
            and self.own > 0
            and self.chunk % 128 == 0
            and self.rows % 8 == 0
            and STEP % self.rows == 0
            and self.rows % c == 0
            and self.all_rows % STEP == 0
            and self.right_rows % 16 == 0
            and self.width % LANES == 0
            and self.mix % 128 == 0
            and self.chunk % self.mix == 0
        )


def prep_kernel(plan, split, x_ref, *rest):
    c, s = plan.ch, plan.seq
    count = s if split else 1
    outs, shares, (turned, share_sem, piece_sem) = rest[:count], rest[count : count + c], rest[-3:]
    me, y = lax.axis_index("seq"), lax.axis_index("ch")
    a = pl.program_id(0)
    value = x_ref[...].T
    turned[a] = value
    if not split:
        outs[0][...] = value.reshape(s, 1, plan.own, plan.width)

    def rows_of(m):
        who = jnp.bitwise_xor(me, m)
        return pl.ds(pl.multiple_of(who * plan.own, plan.own), plan.own)

    if split:
        for m in range(s):
            pltpu.make_async_copy(
                turned.at[a, rows_of(m), :], outs[m].at[a], piece_sem.at[m]
            ).start()

    @pl.when(a == plan.rows - 1)
    def _():
        copies = [
            pltpu.make_async_copy(
                turned.at[pl.ds(jnp.bitwise_xor(y, m) * plan.out_rows, plan.out_rows)],
                shares[m],
                share_sem.at[m],
            )
            for m in range(c)
        ]
        for copy in copies:
            copy.start()
        if split:
            for m in range(s):
                pltpu.make_async_copy(
                    turned.at[:, rows_of(m), :], outs[m], piece_sem.at[m]
                ).wait()
        for copy in copies:
            copy.wait()


def prep(plan, tokens, chunk, split):
    share = jax.ShapeDtypeStruct((plan.out_rows, plan.chunk, plan.width), jnp.bfloat16)
    if split:
        shape = (plan.rows, plan.own, plan.width)
        count, spec = plan.seq, ANY
    else:
        shape = (plan.seq, plan.rows, plan.own, plan.width)
        count = 1
        spec = pl.BlockSpec((plan.seq, 1, plan.own, plan.width), lambda a: (0, a, 0, 0))
    out = pl.pallas_call(
        functools.partial(prep_kernel, plan, split),
        out_shape=[jax.ShapeDtypeStruct(shape, jnp.bfloat16)] * count + [share] * plan.ch,
        grid=(plan.rows,),
        in_specs=[pl.BlockSpec((plan.width, plan.chunk), lambda a: (a, chunk))],
        out_specs=[spec] * count + [ANY] * plan.ch,
        scratch_shapes=[
            pltpu.VMEM((plan.rows, plan.chunk, plan.width), jnp.bfloat16),
            pltpu.SemaphoreType.DMA((plan.ch,)),
            pltpu.SemaphoreType.DMA((plan.seq,)),
        ],
        cost_estimate=pl.CostEstimate(
            flops=0,
            bytes_accessed=6 * plan.rows * plan.chunk * plan.width,
            transcendentals=0,
        ),
        name="prep",
    )(tokens)
    return out[:count], out[count:]


def sections_kernel(plan, count, *refs):
    near, far, own = plan.near, plan.seq // plan.near, plan.own
    pieces, gathered, left = refs[:count], refs[count : count + near], refs[count + near]
    out, x, right, twiddle, first, mixed, sem_x, sem_r, sem_t = refs[count + near + 1 :]
    me = lax.axis_index("seq")
    if count == 1:
        copies = [pltpu.make_async_copy(pieces[0], x, sem_x.at[0])]
    else:
        copies = [
            pltpu.make_async_copy(
                pieces[m], x.at[pl.ds(jnp.bitwise_xor(me, m) * plan.rows, plan.rows)], sem_x.at[m]
            )
            for m in range(count)
        ]
    for m in range(near):
        for n in range(far):
            who = jnp.bitwise_xor(me, n * near + m)
            at = pl.ds(pl.multiple_of(who * plan.right_rows, plan.right_rows), plan.right_rows)
            source = gathered[m].at[n]
            copies.append(
                pltpu.make_async_copy(
                    source.at[pl.ds(0, plan.right_rows)], right.at[at], sem_r.at[m * far + n]
                )
            )
            copies.append(
                pltpu.make_async_copy(
                    source.at[pl.ds(plan.right_rows, plan.rows)],
                    twiddle.at[who],
                    sem_t.at[m * far + n],
                )
            )
    kt = pl.program_id(0)

    @pl.when(kt == 0)
    def _():
        for copy in copies:
            copy.start()
        for copy in copies:
            copy.wait()

    ks = pl.ds(pl.multiple_of(kt * LANES, LANES), LANES)

    def section_one(t, carry):
        rows = x[pl.ds(t * STEP, STEP)].reshape(STEP * own, plan.width)
        value = jnp.dot(rows, right[:, ks], preferred_element_type=jnp.float32)
        value = value.reshape(STEP, own, LANES)
        group = STEP // plan.rows
        factor = twiddle[pl.ds(t * group, group), :, ks].astype(jnp.float32)
        value = value * factor.reshape(STEP, LANES)[:, None, :]
        at = pl.ds(pl.multiple_of(t * STEP, STEP), STEP)
        first[:, at, :] = jnp.swapaxes(value, 0, 1).astype(jnp.bfloat16)
        return carry

    lax.fori_loop(0, plan.all_rows // STEP, section_one, 0)
    for q in range(own):
        mixed[q] = jnp.dot(left[...], first[q], preferred_element_type=jnp.float32)

    def turn(t, carry):
        at = pl.ds(pl.multiple_of(t * STEP, STEP), STEP)
        value = jnp.swapaxes(mixed[:, at, :], 0, 1)
        out[pl.ds(t * STEP, STEP)] = value.astype(jnp.bfloat16)
        return carry

    lax.fori_loop(0, plan.all_rows // STEP, turn, 0)


def sections(plan, pieces, gathered, left):
    s, own, width, bf16 = plan.seq, plan.own, plan.width, jnp.bfloat16
    flops = 2 * plan.all_rows * own * width * (width + plan.all_rows)
    return pl.pallas_call(
        functools.partial(sections_kernel, plan, len(pieces)),
        out_shape=jax.ShapeDtypeStruct((plan.all_rows, own, width), bf16),
        grid=(width // LANES,),
        in_specs=[ANY] * (len(pieces) + len(gathered)) + [VMEM],
        out_specs=pl.BlockSpec((plan.all_rows, own, LANES), lambda k: (0, 0, k)),
        scratch_shapes=[
            pltpu.VMEM((plan.all_rows, own, width), bf16),
            pltpu.VMEM((s * plan.right_rows, width), bf16),
            pltpu.VMEM((s, plan.rows, width), bf16),
            pltpu.VMEM((own, plan.all_rows, LANES), bf16),
            pltpu.VMEM((own, plan.all_rows, LANES), jnp.float32),
            pltpu.SemaphoreType.DMA((s,)),
            pltpu.SemaphoreType.DMA((s,)),
            pltpu.SemaphoreType.DMA((s,)),
        ],
        cost_estimate=pl.CostEstimate(
            flops=flops,
            bytes_accessed=4 * plan.all_rows * own * width + 2 * width * width,
            transcendentals=0,
        ),
        name="sections",
    )(*pieces, *gathered, left)


def load_chunk(plan, piece, shares, mixed, inputs, sem_m, sem_i):
    s, c, own = plan.seq, plan.ch, plan.own
    y = lax.axis_index("ch")
    for r in range(plan.out_rows):
        for n in range(c):
            at = pl.ds(jnp.bitwise_xor(y, n) * plan.chunk, plan.chunk)
            pltpu.make_async_copy(shares[n].at[r], inputs.at[r, at], sem_i.at[r]).start()
        for m in range(s * c):
            row = (m % c) * plan.chunk + (m // c) * own
            pltpu.make_async_copy(
                piece.at[m, r], mixed.at[r, pl.ds(row, own)], sem_m.at[r]
            ).start()


def gate_tile(plan, mixed, inputs, i, ks):
    total = jnp.zeros((1, LANES), jnp.float32)
    for j in range(plan.chunk * plan.ch // plan.mix):
        rs = pl.ds(j * plan.mix, plan.mix)
        value = mixed[i, rs, ks].astype(jnp.float32)
        gate = inputs[i, rs, ks].astype(jnp.float32)
        gated = (value * (gate / (1.0 + jnp.exp(-gate)))).astype(jnp.bfloat16)
        mixed[i, rs, ks] = gated
        gated = gated.astype(jnp.float32)
        total = total + jnp.sum(gated * gated, axis=0, keepdims=True)
    return total


def columns(plan, chunk, j):
    return (j * plan.mix // plan.chunk) * plan.local + chunk * plan.chunk + (
        j * plan.mix % plan.chunk
    )


def turn_dot(value, weight):
    return lax.dot_general(
        value, weight, (((0,), (0,)), ((), ())), preferred_element_type=jnp.float32
    )


def gate_kernel(plan, *refs):
    c = plan.ch
    piece, shares = refs[0], refs[1 : 1 + c]
    gain, weight, out, totals, mixed, inputs, sem_m, sem_i = refs[1 + c :]
    i = pl.program_id(0)

    @pl.when(i == 0)
    def _():
        load_chunk(plan, piece, shares, mixed, inputs, sem_m, sem_i)

    pltpu.make_async_copy(inputs.at[i], inputs.at[i], sem_i.at[i]).wait()
    pltpu.make_async_copy(mixed.at[i], mixed.at[i], sem_m.at[i]).wait()

    def tile(kt, carry):
        ks = pl.ds(pl.multiple_of(kt * LANES, LANES), LANES)
        total = gate_tile(plan, mixed, inputs, i, ks)
        totals[0, :, ks] = jnp.broadcast_to(total, (8, LANES))
        for j in range(plan.chunk * c // plan.mix):
            col = columns(plan, 0, j)
            value = mixed[i, pl.ds(j * plan.mix, plan.mix), ks].astype(jnp.float32)
            value = (value * gain[pl.ds(col, plan.mix), :]).astype(jnp.bfloat16)
            out[ks, pl.ds(j * plan.mix, plan.mix)] = turn_dot(value, weight[col // plan.mix])
        return carry

    lax.fori_loop(0, plan.width // LANES, tile, 0)


def final_kernel(plan, *refs):
    c = plan.ch
    piece, shares = refs[0], refs[1 : 1 + c]
    held, before, gain, weight, out, mixed, inputs, sem_m, sem_i = refs[1 + c :]
    i = pl.program_id(0)

    @pl.when(i == 0)
    def _():
        load_chunk(plan, piece, shares, mixed, inputs, sem_m, sem_i)

    pltpu.make_async_copy(inputs.at[i], inputs.at[i], sem_i.at[i]).wait()
    pltpu.make_async_copy(mixed.at[i], mixed.at[i], sem_m.at[i]).wait()

    def tile(kt, carry):
        ks = pl.ds(pl.multiple_of(kt * LANES, LANES), LANES)
        total = gate_tile(plan, mixed, inputs, i, ks) + before[0, pl.ds(0, 1), ks]
        inverse = lax.rsqrt(total * (1.0 / plan.channels) + 1e-05)
        for j in range(plan.chunk * c // plan.mix):
            col = columns(plan, 1, j)
            value = mixed[i, pl.ds(j * plan.mix, plan.mix), ks].astype(jnp.float32)
            value = (value * inverse * gain[pl.ds(col, plan.mix), :]).astype(jnp.bfloat16)
            result = turn_dot(value, weight[col // plan.mix])
            out[ks, pl.ds(col, plan.mix)] = result.astype(jnp.bfloat16)
        scale = jnp.broadcast_to(inverse, (128, LANES)).T
        for j in range(plan.chunk * c // 128):
            result = held[ks, pl.ds(j * 128, 128)] * scale
            col = (j * 128 // plan.chunk) * plan.local + j * 128 % plan.chunk
            out[ks, pl.ds(col, 128)] = result.astype(jnp.bfloat16)
        return carry

    lax.fori_loop(0, plan.width // LANES, tile, 0)


def tail_scratch(plan):
    shape = (plan.out_rows, plan.chunk * plan.ch, plan.width)
    return [
        pltpu.VMEM(shape, jnp.bfloat16),
        pltpu.VMEM(shape, jnp.bfloat16),
        pltpu.SemaphoreType.DMA((plan.out_rows,)),
        pltpu.SemaphoreType.DMA((plan.out_rows,)),
    ]


def gate(plan, piece, shares, gain, weight):
    size, part = plan.out_rows * plan.width, plan.chunk * plan.ch
    return pl.pallas_call(
        functools.partial(gate_kernel, plan),
        out_shape=[
            jax.ShapeDtypeStruct((size, part), jnp.float32),
            jax.ShapeDtypeStruct((plan.out_rows, 8, plan.width), jnp.float32),
        ],
        grid=(plan.out_rows,),
        in_specs=[ANY] * (1 + plan.ch) + [VMEM, VMEM],
        out_specs=[
            pl.BlockSpec((plan.width, part), lambda i: (i, 0)),
            pl.BlockSpec((1, 8, plan.width), lambda i: (i, 0, 0)),
        ],
        scratch_shapes=tail_scratch(plan),
        cost_estimate=pl.CostEstimate(
            flops=2 * size * part * plan.mix,
            bytes_accessed=8 * size * part,
            transcendentals=size * part,
        ),
        name="gate",
    )(piece, *shares, gain, weight)


def final(plan, piece, shares, held, before, gain, weight):
    size, part = plan.out_rows * plan.width, plan.chunk * plan.ch
    return pl.pallas_call(
        functools.partial(final_kernel, plan),
        out_shape=jax.ShapeDtypeStruct((size, plan.channels), jnp.bfloat16),
        grid=(plan.out_rows,),
        in_specs=[ANY] * (1 + plan.ch)
        + [
            pl.BlockSpec((plan.width, part), lambda i: (i, 0)),
            pl.BlockSpec((1, 8, plan.width), lambda i: (i, 0, 0)),
            VMEM,
            VMEM,
        ],
        out_specs=pl.BlockSpec((plan.width, plan.channels), lambda i: (i, 0)),
        scratch_shapes=tail_scratch(plan),
        cost_estimate=pl.CostEstimate(
            flops=2 * size * part * plan.mix,
            bytes_accessed=10 * size * part,
            transcendentals=size * part,
        ),
        name="final",
    )(piece, *shares, held, before, gain, weight)


def swap(value, mask, axis):
    count = lax.axis_size(axis)
    return lax.ppermute(value, axis, [(i, i ^ mask) for i in range(count)])


def exchange(value, axes):
    return lax.all_to_all(value, axes, split_axis=0, concat_axis=0, tiled=True)


def chunked_body(plan, tokens, right_block, twiddle, left_block, gain, mix_weight):
    s, c, near, own = plan.seq, plan.ch, plan.near, plan.own
    pad = plan.gather_rows - right_block.shape[0] - twiddle.shape[0]
    zeros = jnp.zeros((pad, plan.width), jnp.bfloat16)
    held = jnp.concatenate([right_block, twiddle, zeros], axis=0)[None]
    gain = jnp.broadcast_to(gain[:, None], (plan.channels, LANES))
    column = [held]
    for n in range(1, s // near):
        column.append(swap(held, n * near, "seq"))
    column = jnp.concatenate(column, axis=0)
    gathered = [column]
    for m in range(1, near):
        gathered.append(swap(column, m, "seq"))
    arrived, shares = [], []
    for k in range(CHUNKS):
        pieces, share = prep(plan, tokens, k, k == 1)
        if k == 0:
            block = exchange(pieces[0], "seq")
            arrived.append([block.reshape(plan.all_rows, own, plan.width)])
        else:
            arrived.append([pieces[0]] + [None] * (s - 1))
            for m in reversed(range(1, s)):
                arrived[k][m] = swap(pieces[m], m, "seq")
        shares.append([share[0]])
        for n in range(1, c):
            shares[k].append(swap(share[n], n, "ch"))
    landed = []
    for k in range(CHUNKS):
        out = sections(plan, arrived[k], gathered, left_block)
        out = out.reshape(s * c, plan.out_rows, own, plan.width)
        landed.append(exchange(out, ("seq", "ch")))
    held, before = gate(plan, landed[0], shares[0], gain, mix_weight)
    return final(plan, landed[1], shares[1], held, before, gain, mix_weight)


def plain_body(tokens, right_block, twiddle, left_block, gain, mix_weight):
    row_width = right_block.shape[1]
    row_count = tokens.shape[0] // row_width
    local_width = tokens.shape[1]
    inputs = tokens.reshape(row_count, row_width, local_width)
    whole_right = lax.all_gather(right_block, "seq", axis=0, tiled=True)
    first_section = jnp.einsum(
        "abc,bk->akc", inputs, whole_right, preferred_element_type=jnp.float32
    )
    spread = (first_section * twiddle.astype(jnp.float32)[:, :, None]).astype(jnp.bfloat16)
    mixed_rows = jnp.einsum(
        "ij,jbc->ibc",
        left_block,
        lax.all_to_all(spread, "seq", split_axis=1, concat_axis=0, tiled=True),
        preferred_element_type=jnp.float32,
    ).astype(jnp.bfloat16)
    sequence_mixed = lax.all_to_all(mixed_rows, "seq", split_axis=0, concat_axis=1, tiled=True)
    gated = (sequence_mixed.astype(jnp.float32) * jax.nn.silu(inputs.astype(jnp.float32))).astype(
        jnp.bfloat16
    )
    ch_count = lax.axis_size("ch")
    pieces = gated.reshape(ch_count, row_count * row_width // ch_count, local_width)
    shard_piece = lax.all_to_all(pieces, "ch", split_axis=0, concat_axis=2, tiled=True)
    values = shard_piece.astype(jnp.float32)
    inverse_rms = lax.rsqrt(jnp.mean(values * values, axis=-1, keepdims=True) + 1e-05)
    normed = (values * inverse_rms * gain).astype(jnp.bfloat16)
    block_count = mix_weight.shape[0]
    block_width = mix_weight.shape[1]
    normed = normed.reshape(shard_piece.shape[0], shard_piece.shape[1], block_count, block_width)
    result = jnp.einsum("otki,kij->otkj", normed, mix_weight, preferred_element_type=jnp.float32)
    mixed_out = result.astype(jnp.bfloat16).reshape(shard_piece.shape)
    return mixed_out.reshape(mixed_out.shape[1], mixed_out.shape[2])


def body(tokens, right_block, twiddle, left_block, gain, mix_weight):
    plan = Plan(tokens, right_block, twiddle, left_block, mix_weight)
    if plan.fits():
        return chunked_body(plan, tokens, right_block, twiddle, left_block, gain, mix_weight)
    return plain_body(tokens, right_block, twiddle, left_block, gain, mix_weight)


def solution(mesh):
    in_specs = (P("seq", "ch"), P("seq", None), P("seq", None), P(), P(), P())
    out_specs = P(("seq", "ch"), None)
    return jax.shard_map(body, mesh=mesh, in_specs=in_specs, out_specs=out_specs, check_vma=False)
```

```python
import functools

import jax
import jax.numpy as jnp
from jax import lax
from jax.experimental import pallas as pl
from jax.experimental.pallas import tpu as pltpu
from jax.sharding import PartitionSpec as P


ANY = pl.BlockSpec(memory_space=pl.ANY)
VMEM = pl.BlockSpec(memory_space=pltpu.VMEM)
LANES = 256
CHUNKS = 2
STEP = 16


class Plan:
    def __init__(self, tokens, right_block, twiddle, left_block, mix_weight):
        self.seq = lax.axis_size("seq")
        self.ch = lax.axis_size("ch")
        self.width = right_block.shape[1]
        self.rows = tokens.shape[0] // self.width
        self.local = tokens.shape[1]
        self.right_rows = right_block.shape[0]
        self.all_rows = left_block.shape[0]
        self.chunk = self.local // CHUNKS
        self.own = self.chunk // self.seq
        self.out_rows = self.rows // self.ch
        self.channels = self.local * self.ch
        self.mix = mix_weight.shape[1]
        self.near = 1
        while self.near * self.near < self.seq:
            self.near *= 2
        pad = self.right_rows + twiddle.shape[0]
        self.gather_rows = pad + (-pad) % 16

    def fits(self):
        s, c = self.seq, self.ch
        return (
            s > 1
            and s <= 16
            and c > 1
            and c <= 4
            and s & (s - 1) == 0
            and c & (c - 1) == 0
            and self.own % 16 == 0
            and self.own > 0
            and self.chunk % 128 == 0
            and self.rows % 8 == 0
            and STEP % self.rows == 0
            and self.rows % c == 0
            and self.all_rows % STEP == 0
            and self.right_rows % 16 == 0
            and self.width % LANES == 0
            and self.mix % 128 == 0
            and self.chunk % self.mix == 0
        )


def prep_kernel(plan, chunk, split, x_ref, *rest):
    s = plan.seq
    count = s if split else 1
    outs, shares = rest[:count], rest[count:-5]
    given, turned, in_sem, out_sem, share_sem = rest[-5:]
    me, y = lax.axis_index("seq"), lax.axis_index("ch")
    loads = [
        pltpu.make_async_copy(
            x_ref.at[pl.ds(a * plan.width, plan.width), pl.ds(chunk * plan.chunk, plan.chunk)],
            given.at[a],
            in_sem.at[a],
        )
        for a in range(plan.rows)
    ]
    for load in loads:
        load.start()
    stores = []
    for a in range(plan.rows):
        loads[a].wait()
        turned[a] = given[a].T.reshape(s, plan.own, plan.width)
        if split:
            for m in range(s):
                pltpu.make_async_copy(
                    turned.at[a, jnp.bitwise_xor(me, m)], outs[m].at[a], out_sem.at[m]
                ).start()
        else:
            stores.append(
                pltpu.make_async_copy(turned.at[a], outs[0].at[:, a], out_sem.at[a])
            )
            stores[-1].start()
    for m in range(len(shares)):
        at = pl.ds(jnp.bitwise_xor(y, m) * plan.out_rows, plan.out_rows)
        stores.append(pltpu.make_async_copy(turned.at[at], shares[m], share_sem.at[m]))
        stores[-1].start()
    if split:
        for m in range(s):
            pltpu.make_async_copy(
                turned.at[:, jnp.bitwise_xor(me, m)], outs[m], out_sem.at[m]
            ).wait()
    for store in stores:
        store.wait()


def prep(plan, tokens, chunk, split):
    bf16 = jnp.bfloat16
    if split:
        shapes = [jax.ShapeDtypeStruct((plan.rows, plan.own, plan.width), bf16)] * plan.seq
        shape = (plan.out_rows, plan.seq, plan.own, plan.width)
        shapes += [jax.ShapeDtypeStruct(shape, bf16)] * plan.ch
    else:
        shape = (plan.seq, plan.rows, plan.own, plan.width)
        shapes = [jax.ShapeDtypeStruct(shape, bf16)]
    out = pl.pallas_call(
        functools.partial(prep_kernel, plan, chunk, split),
        out_shape=shapes,
        in_specs=[ANY],
        out_specs=[ANY] * len(shapes),
        scratch_shapes=[
            pltpu.VMEM((plan.rows, plan.width, plan.chunk), bf16),
            pltpu.VMEM((plan.rows, plan.seq, plan.own, plan.width), bf16),
            pltpu.SemaphoreType.DMA((plan.rows,)),
            pltpu.SemaphoreType.DMA((max(plan.seq, plan.rows),)),
            pltpu.SemaphoreType.DMA((plan.ch,)),
        ],
        cost_estimate=pl.CostEstimate(
            flops=0,
            bytes_accessed=6 * plan.rows * plan.chunk * plan.width,
            transcendentals=0,
        ),
        name="prep",
    )(tokens)
    if split:
        shape = (plan.out_rows, plan.chunk, plan.width)
        return out[: plan.seq], [share.reshape(shape) for share in out[plan.seq :]]
    return out[0], [own_rows(plan, out[0], n) for n in range(plan.ch)]


def own_rows(plan, block, mask):
    start = jnp.bitwise_xor(lax.axis_index("ch"), mask) * plan.out_rows
    part = lax.dynamic_slice_in_dim(block, start, plan.out_rows, axis=1)
    return part.transpose(1, 0, 2, 3).reshape(plan.out_rows, plan.chunk, plan.width)


def sections_kernel(plan, count, *refs):
    near, far, own = plan.near, plan.seq // plan.near, plan.own
    pieces, gathered, left = refs[:count], refs[count : count + near], refs[count + near]
    out, x, right, twiddle, first, mixed, sem_x, sem_r, sem_t = refs[count + near + 1 :]
    me = lax.axis_index("seq")
    if count == 1:
        copies = [pltpu.make_async_copy(pieces[0], x, sem_x.at[0])]
    else:
        copies = [
            pltpu.make_async_copy(
                pieces[m], x.at[pl.ds(jnp.bitwise_xor(me, m) * plan.rows, plan.rows)], sem_x.at[m]
            )
            for m in range(count)
        ]
    for m in range(near):
        for n in range(far):
            who = jnp.bitwise_xor(me, n * near + m)
            at = pl.ds(pl.multiple_of(who * plan.right_rows, plan.right_rows), plan.right_rows)
            source = gathered[m].at[n]
            copies.append(
                pltpu.make_async_copy(
                    source.at[pl.ds(0, plan.right_rows)], right.at[at], sem_r.at[m * far + n]
                )
            )
            copies.append(
                pltpu.make_async_copy(
                    source.at[pl.ds(plan.right_rows, plan.rows)],
                    twiddle.at[who],
                    sem_t.at[m * far + n],
                )
            )
    kt = pl.program_id(0)

    @pl.when(kt == 0)
    def _():
        for copy in copies:
            copy.start()
        for copy in copies:
            copy.wait()

    ks = pl.ds(pl.multiple_of(kt * LANES, LANES), LANES)

    def section_one(t, carry):
        rows = x[pl.ds(t * STEP, STEP)].reshape(STEP * own, plan.width)
        value = jnp.dot(rows, right[:, ks], preferred_element_type=jnp.float32)
        value = value.reshape(STEP, own, LANES)
        group = STEP // plan.rows
        factor = twiddle[pl.ds(t * group, group), :, ks].astype(jnp.float32)
        value = value * factor.reshape(STEP, LANES)[:, None, :]
        at = pl.ds(pl.multiple_of(t * STEP, STEP), STEP)
        first[:, at, :] = jnp.swapaxes(value, 0, 1).astype(jnp.bfloat16)
        return carry

    lax.fori_loop(0, plan.all_rows // STEP, section_one, 0)
    for q in range(own):
        mixed[q] = jnp.dot(left[...], first[q], preferred_element_type=jnp.float32)

    def turn(t, carry):
        at = pl.ds(pl.multiple_of(t * STEP, STEP), STEP)
        value = jnp.swapaxes(mixed[:, at, :], 0, 1)
        out[pl.ds(t * STEP, STEP)] = value.astype(jnp.bfloat16)
        return carry

    lax.fori_loop(0, plan.all_rows // STEP, turn, 0)


def sections(plan, pieces, gathered, left):
    s, own, width, bf16 = plan.seq, plan.own, plan.width, jnp.bfloat16
    flops = 2 * plan.all_rows * own * width * (width + plan.all_rows)
    return pl.pallas_call(
        functools.partial(sections_kernel, plan, len(pieces)),
        out_shape=jax.ShapeDtypeStruct((plan.all_rows, own, width), bf16),
        grid=(width // LANES,),
        in_specs=[ANY] * (len(pieces) + len(gathered)) + [VMEM],
        out_specs=pl.BlockSpec((plan.all_rows, own, LANES), lambda k: (0, 0, k)),
        scratch_shapes=[
            pltpu.VMEM((plan.all_rows, own, width), bf16),
            pltpu.VMEM((s * plan.right_rows, width), bf16),
            pltpu.VMEM((s, plan.rows, width), bf16),
            pltpu.VMEM((own, plan.all_rows, LANES), bf16),
            pltpu.VMEM((own, plan.all_rows, LANES), jnp.float32),
            pltpu.SemaphoreType.DMA((s,)),
            pltpu.SemaphoreType.DMA((s,)),
            pltpu.SemaphoreType.DMA((s,)),
        ],
        cost_estimate=pl.CostEstimate(
            flops=flops,
            bytes_accessed=4 * plan.all_rows * own * width + 2 * width * width,
            transcendentals=0,
        ),
        name="sections",
    )(*pieces, *gathered, left)


def load_piece(plan, piece, mixed, sem):
    for r in range(plan.out_rows):
        for m in range(plan.seq * plan.ch):
            row = (m % plan.ch) * plan.chunk + (m // plan.ch) * plan.own
            pltpu.make_async_copy(
                piece.at[m, r], mixed.at[r, pl.ds(row, plan.own)], sem.at[r]
            ).start()


def load_shares(plan, shares, inputs, sem):
    y = lax.axis_index("ch")
    for r in range(plan.out_rows):
        for n in range(plan.ch):
            at = pl.ds(jnp.bitwise_xor(y, n) * plan.chunk, plan.chunk)
            pltpu.make_async_copy(shares[n].at[r], inputs.at[r, at], sem.at[r]).start()


def wait_row(buffer, sem, r):
    pltpu.make_async_copy(buffer.at[r], buffer.at[r], sem.at[r]).wait()


def column(plan, chunk, j):
    row = j * plan.mix
    return (row // plan.chunk) * plan.local + chunk * plan.chunk + row % plan.chunk


def silu(value):
    return value / (1.0 + jnp.exp(-value))


def turn_dot(value, weight):
    return lax.dot_general(
        value, weight, (((0,), (0,)), ((), ())), preferred_element_type=jnp.float32
    )


def gate_kernel(plan, *refs):
    c = plan.ch
    piece, shares, later = refs[0], refs[1 : 1 + c], refs[1 + c : 1 + 2 * c]
    gain, weight, out, gates, totals = refs[1 + 2 * c : 6 + 2 * c]
    mixed, inputs, after, sem_m, sem_i, sem_a = refs[6 + 2 * c :]
    i = pl.program_id(0)

    @pl.when(i == 0)
    def _():
        load_shares(plan, later, after, sem_a)
        load_shares(plan, shares, inputs, sem_i)
        load_piece(plan, piece, mixed, sem_m)

    wait_row(after, sem_a, i)
    wait_row(inputs, sem_i, i)
    wait_row(mixed, sem_m, i)

    def tile(kt, carry):
        ks = pl.ds(pl.multiple_of(kt * LANES, LANES), LANES)
        total = jnp.zeros((1, LANES), jnp.float32)
        for j in range(plan.chunk * c // plan.mix):
            rs = pl.ds(j * plan.mix, plan.mix)
            gates[0, rs, ks] = silu(after[i, rs, ks].astype(jnp.float32)).astype(jnp.bfloat16)
            value = mixed[i, rs, ks].astype(jnp.float32)
            value = value * silu(inputs[i, rs, ks].astype(jnp.float32))
            value = value.astype(jnp.bfloat16).astype(jnp.float32)
            total = total + jnp.sum(value * value, axis=0, keepdims=True)
            col = column(plan, 0, j)
            value = (value * gain[pl.ds(col, plan.mix), :]).astype(jnp.bfloat16)
            out[ks, rs] = turn_dot(value, weight[col // plan.mix]).astype(jnp.bfloat16)
        totals[0, :, ks] = jnp.broadcast_to(total, (8, LANES))
        return carry

    lax.fori_loop(0, plan.width // LANES, tile, 0)


def final_kernel(plan, *refs):
    piece, gates, held, before, gain, weight, result = refs[:7]
    mixed, inputs, left, out, sem_m, sem_i, sem_h, sem_o = refs[7:]
    c, width = plan.ch, plan.width
    for r in range(plan.out_rows):
        pltpu.make_async_copy(gates.at[r], inputs.at[r], sem_i.at[r]).start()
        at = pl.ds(r * width, width)
        pltpu.make_async_copy(held.at[at], left.at[r], sem_h.at[r]).start()
    load_piece(plan, piece, mixed, sem_m)
    stores = []
    for r in range(plan.out_rows):
        wait_row(mixed, sem_m, r)
        wait_row(inputs, sem_i, r)
        wait_row(left, sem_h, r)

        def tile(kt, carry):
            ks = pl.ds(pl.multiple_of(kt * LANES, LANES), LANES)
            total = before[r, pl.ds(0, 1), ks]
            parts = []
            for j in range(plan.chunk * c // plan.mix):
                rs = pl.ds(j * plan.mix, plan.mix)
                value = mixed[r, rs, ks].astype(jnp.float32)
                value = value * inputs[r, rs, ks].astype(jnp.float32)
                total = total + jnp.sum(value * value, axis=0, keepdims=True)
                col = column(plan, 1, j)
                value = (value * gain[pl.ds(col, plan.mix), :]).astype(jnp.bfloat16)
                parts.append((col, turn_dot(value, weight[col // plan.mix])))
            inverse = lax.rsqrt(total * (1.0 / plan.channels) + 1e-05)
            scale = jnp.broadcast_to(inverse, (128, LANES)).T
            for col, part in parts:
                for q in range(plan.mix // 128):
                    value = part[:, q * 128 : (q + 1) * 128] * scale
                    out[r, ks, pl.ds(col + q * 128, 128)] = value.astype(jnp.bfloat16)
            for j in range(plan.chunk * c // 128):
                value = left[r, ks, pl.ds(j * 128, 128)].astype(jnp.float32) * scale
                col = (j * 128 // plan.chunk) * plan.local + j * 128 % plan.chunk
                out[r, ks, pl.ds(col, 128)] = value.astype(jnp.bfloat16)
            return carry

        lax.fori_loop(0, width // LANES, tile, 0)
        stores.append(
            pltpu.make_async_copy(out.at[r], result.at[pl.ds(r * width, width)], sem_o.at[r])
        )
        stores[-1].start()
    for store in stores:
        store.wait()


def gate(plan, piece, shares, later, gain, weight):
    size, part = plan.out_rows * plan.width, plan.chunk * plan.ch
    shape, bf16 = (plan.out_rows, part, plan.width), jnp.bfloat16
    sem = pltpu.SemaphoreType.DMA((plan.out_rows,))
    return pl.pallas_call(
        functools.partial(gate_kernel, plan),
        out_shape=[
            jax.ShapeDtypeStruct((size, part), bf16),
            jax.ShapeDtypeStruct(shape, bf16),
            jax.ShapeDtypeStruct((plan.out_rows, 8, plan.width), jnp.float32),
        ],
        grid=(plan.out_rows,),
        in_specs=[ANY] * (1 + 2 * plan.ch) + [VMEM, VMEM],
        out_specs=[
            pl.BlockSpec((plan.width, part), lambda i: (i, 0)),
            pl.BlockSpec((1, part, plan.width), lambda i: (i, 0, 0)),
            pl.BlockSpec((1, 8, plan.width), lambda i: (i, 0, 0)),
        ],
        scratch_shapes=[pltpu.VMEM(shape, bf16)] * 3 + [sem] * 3,
        cost_estimate=pl.CostEstimate(
            flops=2 * size * part * plan.mix,
            bytes_accessed=10 * size * part,
            transcendentals=2 * size * part,
        ),
        name="gate",
    )(piece, *shares, *later, gain, weight)


def final(plan, piece, gates, held, before, gain, weight):
    size, part = plan.out_rows * plan.width, plan.chunk * plan.ch
    shape, bf16 = (plan.out_rows, part, plan.width), jnp.bfloat16
    sem = pltpu.SemaphoreType.DMA((plan.out_rows,))
    return pl.pallas_call(
        functools.partial(final_kernel, plan),
        out_shape=jax.ShapeDtypeStruct((size, plan.channels), bf16),
        in_specs=[ANY] * 3 + [VMEM] * 3,
        out_specs=ANY,
        scratch_shapes=[
            pltpu.VMEM(shape, bf16),
            pltpu.VMEM(shape, bf16),
            pltpu.VMEM((plan.out_rows, plan.width, part), bf16),
            pltpu.VMEM((plan.out_rows, plan.width, plan.channels), bf16),
        ]
        + [sem] * 4,
        cost_estimate=pl.CostEstimate(
            flops=2 * size * part * plan.mix,
            bytes_accessed=10 * size * part,
            transcendentals=0,
        ),
        name="final",
    )(piece, gates, held, before, gain, weight)


def swap(value, mask, axis):
    count = lax.axis_size(axis)
    return lax.ppermute(value, axis, [(i, i ^ mask) for i in range(count)])


def exchange(value, axes):
    return lax.all_to_all(value, axes, split_axis=0, concat_axis=0, tiled=True)


def chunked_body(plan, tokens, right_block, twiddle, left_block, gain, mix_weight):
    s, c, near, own = plan.seq, plan.ch, plan.near, plan.own
    pad = plan.gather_rows - right_block.shape[0] - twiddle.shape[0]
    zeros = jnp.zeros((pad, plan.width), jnp.bfloat16)
    held = jnp.concatenate([right_block, twiddle, zeros], axis=0)[None]
    gain = jnp.broadcast_to(gain[:, None], (plan.channels, LANES))
    column = [held]
    for n in range(1, s // near):
        column.append(swap(held, n * near, "seq"))
    column = jnp.concatenate(column, axis=0)
    gathered = [column]
    for m in range(1, near):
        gathered.append(swap(column, m, "seq"))
    arrived, shares = [], []
    for k in range(CHUNKS):
        pieces, share = prep(plan, tokens, k, k == 1)
        if k == 0:
            block = exchange(pieces, "seq")
            arrived.append([block.reshape(plan.all_rows, own, plan.width)])
        else:
            arrived.append([pieces[0]] + [None] * (s - 1))
            for m in reversed(range(1, s)):
                arrived[k][m] = swap(pieces[m], m, "seq")
        shares.append([share[0]])
        for n in range(1, c):
            shares[k].append(swap(share[n], n, "ch"))
    landed = []
    for k in range(CHUNKS):
        out = sections(plan, arrived[k], gathered, left_block)
        out = out.reshape(s * c, plan.out_rows, own, plan.width)
        landed.append(exchange(out, ("seq", "ch")))
    held, gates, before = gate(plan, landed[0], *shares, gain, mix_weight)
    return final(plan, landed[1], gates, held, before, gain, mix_weight)


def plain_body(tokens, right_block, twiddle, left_block, gain, mix_weight):
    row_width = right_block.shape[1]
    row_count = tokens.shape[0] // row_width
    local_width = tokens.shape[1]
    inputs = tokens.reshape(row_count, row_width, local_width)
    whole_right = lax.all_gather(right_block, "seq", axis=0, tiled=True)
    first_section = jnp.einsum(
        "abc,bk->akc", inputs, whole_right, preferred_element_type=jnp.float32
    )
    spread = (first_section * twiddle.astype(jnp.float32)[:, :, None]).astype(jnp.bfloat16)
    mixed_rows = jnp.einsum(
        "ij,jbc->ibc",
        left_block,
        lax.all_to_all(spread, "seq", split_axis=1, concat_axis=0, tiled=True),
        preferred_element_type=jnp.float32,
    ).astype(jnp.bfloat16)
    sequence_mixed = lax.all_to_all(mixed_rows, "seq", split_axis=0, concat_axis=1, tiled=True)
    gated = (sequence_mixed.astype(jnp.float32) * jax.nn.silu(inputs.astype(jnp.float32))).astype(
        jnp.bfloat16
    )
    ch_count = lax.axis_size("ch")
    pieces = gated.reshape(ch_count, row_count * row_width // ch_count, local_width)
    shard_piece = lax.all_to_all(pieces, "ch", split_axis=0, concat_axis=2, tiled=True)
    values = shard_piece.astype(jnp.float32)
    inverse_rms = lax.rsqrt(jnp.mean(values * values, axis=-1, keepdims=True) + 1e-05)
    normed = (values * inverse_rms * gain).astype(jnp.bfloat16)
    block_count = mix_weight.shape[0]
    block_width = mix_weight.shape[1]
    normed = normed.reshape(shard_piece.shape[0], shard_piece.shape[1], block_count, block_width)
    result = jnp.einsum("otki,kij->otkj", normed, mix_weight, preferred_element_type=jnp.float32)
    mixed_out = result.astype(jnp.bfloat16).reshape(shard_piece.shape)
    return mixed_out.reshape(mixed_out.shape[1], mixed_out.shape[2])


def body(tokens, right_block, twiddle, left_block, gain, mix_weight):
    plan = Plan(tokens, right_block, twiddle, left_block, mix_weight)
    if plan.fits():
        return chunked_body(plan, tokens, right_block, twiddle, left_block, gain, mix_weight)
    return plain_body(tokens, right_block, twiddle, left_block, gain, mix_weight)


def solution(mesh):
    in_specs = (P("seq", "ch"), P("seq", None), P("seq", None), P(), P(), P())
    out_specs = P(("seq", "ch"), None)
    return jax.shard_map(body, mesh=mesh, in_specs=in_specs, out_specs=out_specs, check_vma=False)
```

```python
import functools

import jax
import jax.numpy as jnp
from jax import lax
from jax.experimental import pallas as pl
from jax.experimental.pallas import tpu as pltpu
from jax.sharding import PartitionSpec as P


ANY = pl.BlockSpec(memory_space=pl.ANY)
VMEM = pl.BlockSpec(memory_space=pltpu.VMEM)
LANES = 256
CHUNKS = 2
STEP = 16


class Plan:
    def __init__(self, tokens, right_block, twiddle, left_block, mix_weight):
        self.seq = lax.axis_size("seq")
        self.ch = lax.axis_size("ch")
        self.width = right_block.shape[1]
        self.rows = tokens.shape[0] // self.width
        self.local = tokens.shape[1]
        self.right_rows = right_block.shape[0]
        self.all_rows = left_block.shape[0]
        self.chunk = self.local // CHUNKS
        self.own = self.chunk // self.seq
        self.out_rows = self.rows // self.ch
        self.channels = self.local * self.ch
        self.mix = mix_weight.shape[1]
        self.half = self.seq // 2
        self.near = 1
        while self.near * self.near < self.seq:
            self.near *= 2
        pad = self.right_rows + twiddle.shape[0]
        self.gather_rows = pad + (-pad) % 16

    def fits(self):
        s, c = self.seq, self.ch
        return (
            s > 1
            and s <= 16
            and c > 1
            and c <= 4
            and s & (s - 1) == 0
            and c & (c - 1) == 0
            and self.own % 16 == 0
            and self.own > 0
            and self.chunk % 128 == 0
            and self.rows % 8 == 0
            and STEP % self.rows == 0
            and self.rows % c == 0
            and self.all_rows % STEP == 0
            and self.right_rows % 16 == 0
            and self.width % LANES == 0
            and self.mix % 128 == 0
            and self.chunk % self.mix == 0
        )


def prep_kernel(plan, chunk, split, x_ref, *rest):
    s = plan.seq
    count = s if split else 1
    outs, shares = rest[:count], rest[count:-5]
    given, turned, in_sem, out_sem, share_sem = rest[-5:]
    me, y = lax.axis_index("seq"), lax.axis_index("ch")
    loads = [
        pltpu.make_async_copy(
            x_ref.at[pl.ds(a * plan.width, plan.width), pl.ds(chunk * plan.chunk, plan.chunk)],
            given.at[a],
            in_sem.at[a],
        )
        for a in range(plan.rows)
    ]
    for load in loads:
        load.start()
    stores = []
    for a in range(plan.rows):
        loads[a].wait()
        turned[a] = given[a].T.reshape(s, plan.own, plan.width)
        if split:
            for m in range(s):
                pltpu.make_async_copy(
                    turned.at[a, jnp.bitwise_xor(me, m)], outs[m].at[a], out_sem.at[m]
                ).start()
        else:
            stores.append(
                pltpu.make_async_copy(turned.at[a], outs[0].at[:, a], out_sem.at[a])
            )
            stores[-1].start()
    for m in range(len(shares)):
        at = pl.ds(jnp.bitwise_xor(y, m) * plan.out_rows, plan.out_rows)
        stores.append(pltpu.make_async_copy(turned.at[at], shares[m], share_sem.at[m]))
        stores[-1].start()
    if split:
        for m in range(s):
            pltpu.make_async_copy(
                turned.at[:, jnp.bitwise_xor(me, m)], outs[m], out_sem.at[m]
            ).wait()
    for store in stores:
        store.wait()


def prep(plan, tokens, chunk, split):
    bf16 = jnp.bfloat16
    if split:
        shapes = [jax.ShapeDtypeStruct((plan.rows, plan.own, plan.width), bf16)] * plan.seq
        shape = (plan.out_rows, plan.seq, plan.own, plan.width)
        shapes += [jax.ShapeDtypeStruct(shape, bf16)] * plan.ch
    else:
        shape = (plan.seq, plan.rows, plan.own, plan.width)
        shapes = [jax.ShapeDtypeStruct(shape, bf16)]
    out = pl.pallas_call(
        functools.partial(prep_kernel, plan, chunk, split),
        out_shape=shapes,
        in_specs=[ANY],
        out_specs=[ANY] * len(shapes),
        scratch_shapes=[
            pltpu.VMEM((plan.rows, plan.width, plan.chunk), bf16),
            pltpu.VMEM((plan.rows, plan.seq, plan.own, plan.width), bf16),
            pltpu.SemaphoreType.DMA((plan.rows,)),
            pltpu.SemaphoreType.DMA((max(plan.seq, plan.rows),)),
            pltpu.SemaphoreType.DMA((plan.ch,)),
        ],
        cost_estimate=pl.CostEstimate(
            flops=0,
            bytes_accessed=6 * plan.rows * plan.chunk * plan.width,
            transcendentals=0,
        ),
        name="prep",
    )(tokens)
    if split:
        shape = (plan.out_rows, plan.chunk, plan.width)
        return out[: plan.seq], [share.reshape(shape) for share in out[plan.seq :]]
    return out[0], [own_rows(plan, out[0], n) for n in range(plan.ch)]


def own_rows(plan, block, mask):
    start = jnp.bitwise_xor(lax.axis_index("ch"), mask) * plan.out_rows
    part = lax.dynamic_slice_in_dim(block, start, plan.out_rows, axis=1)
    return part.transpose(1, 0, 2, 3).reshape(plan.out_rows, plan.chunk, plan.width)


def sections_kernel(plan, count, split, *refs):
    near, far, own = plan.near, plan.seq // plan.near, plan.own
    pieces, gathered, left = refs[:count], refs[count : count + near], refs[count + near]
    parts = 1 + plan.half * plan.ch if split else 1
    outs = refs[count + near + 1 : count + near + 1 + parts]
    x, right, twiddle, first, mixed, sem_x, sem_r, sem_t, *more = refs[count + near + 1 + parts :]
    out, sem_o = more if split else (outs[0], None)
    me, y = lax.axis_index("seq"), lax.axis_index("ch")
    if count == 1:
        copies = [pltpu.make_async_copy(pieces[0], x, sem_x.at[0])]
    else:
        copies = [
            pltpu.make_async_copy(
                pieces[m], x.at[pl.ds(jnp.bitwise_xor(me, m) * plan.rows, plan.rows)], sem_x.at[m]
            )
            for m in range(count)
        ]
    for m in range(near):
        for n in range(far):
            who = jnp.bitwise_xor(me, n * near + m)
            at = pl.ds(pl.multiple_of(who * plan.right_rows, plan.right_rows), plan.right_rows)
            source = gathered[m].at[n]
            copies.append(
                pltpu.make_async_copy(
                    source.at[pl.ds(0, plan.right_rows)], right.at[at], sem_r.at[m * far + n]
                )
            )
            copies.append(
                pltpu.make_async_copy(
                    source.at[pl.ds(plan.right_rows, plan.rows)],
                    twiddle.at[who],
                    sem_t.at[m * far + n],
                )
            )
    kt = pl.program_id(0)

    @pl.when(kt == 0)
    def _():
        for copy in copies:
            copy.start()
        for copy in copies:
            copy.wait()

    ks = pl.ds(pl.multiple_of(kt * LANES, LANES), LANES)

    def section_one(t, carry):
        rows = x[pl.ds(t * STEP, STEP)].reshape(STEP * own, plan.width)
        value = jnp.dot(rows, right[:, ks], preferred_element_type=jnp.float32)
        value = value.reshape(STEP, own, LANES)
        group = STEP // plan.rows
        factor = twiddle[pl.ds(t * group, group), :, ks].astype(jnp.float32)
        value = value * factor.reshape(STEP, LANES)[:, None, :]
        at = pl.ds(pl.multiple_of(t * STEP, STEP), STEP)
        first[:, at, :] = jnp.swapaxes(value, 0, 1).astype(jnp.bfloat16)
        return carry

    lax.fori_loop(0, plan.all_rows // STEP, section_one, 0)
    for q in range(own):
        mixed[q] = jnp.dot(left[...], first[q], preferred_element_type=jnp.float32)

    def turn(t, carry):
        at = pl.ds(pl.multiple_of(t * STEP, STEP), STEP)
        value = jnp.swapaxes(mixed[:, at, :], 0, 1)
        if split:
            out[pl.ds(t * STEP, STEP), :, ks] = value.astype(jnp.bfloat16)
        else:
            out[pl.ds(t * STEP, STEP)] = value.astype(jnp.bfloat16)
        return carry

    lax.fori_loop(0, plan.all_rows // STEP, turn, 0)
    if split:

        @pl.when(kt == plan.width // LANES - 1)
        def _():
            half = plan.half
            stores = []
            for m in range(half):
                for n in range(plan.ch):
                    row = jnp.bitwise_xor(me, half + m) * plan.rows
                    row = row + jnp.bitwise_xor(y, n) * plan.out_rows
                    stores.append(
                        pltpu.make_async_copy(
                            out.at[pl.ds(row, plan.out_rows)],
                            outs[1 + m * plan.ch + n],
                            sem_o.at[1 + m * plan.ch + n],
                        )
                    )
            rows = half * plan.rows
            stores.append(
                pltpu.make_async_copy(
                    out.at[pl.ds((me // half) * rows, rows)], outs[0], sem_o.at[0]
                )
            )
            for store in stores:
                store.start()
            for store in stores:
                store.wait()


def sections(plan, pieces, gathered, left, split):
    s, own, width, bf16 = plan.seq, plan.own, plan.width, jnp.bfloat16
    flops = 2 * plan.all_rows * own * width * (width + plan.all_rows)
    scratch = []
    if split:
        shapes = [jax.ShapeDtypeStruct((plan.half * plan.rows, own, width), bf16)]
        shapes += [jax.ShapeDtypeStruct((plan.out_rows, own, width), bf16)] * (plan.half * plan.ch)
        specs = [ANY] * len(shapes)
        scratch.append(pltpu.VMEM((plan.all_rows, own, width), bf16))
        scratch.append(pltpu.SemaphoreType.DMA((len(shapes),)))
    else:
        shapes = jax.ShapeDtypeStruct((plan.all_rows, own, width), bf16)
        specs = pl.BlockSpec((plan.all_rows, own, LANES), lambda k: (0, 0, k))
    return pl.pallas_call(
        functools.partial(sections_kernel, plan, len(pieces), split),
        out_shape=shapes,
        grid=(width // LANES,),
        in_specs=[ANY] * (len(pieces) + len(gathered)) + [VMEM],
        out_specs=specs,
        scratch_shapes=[
            pltpu.VMEM((plan.all_rows, own, width), bf16),
            pltpu.VMEM((s * plan.right_rows, width), bf16),
            pltpu.VMEM((s, plan.rows, width), bf16),
            pltpu.VMEM((own, plan.all_rows, LANES), bf16),
            pltpu.VMEM((own, plan.all_rows, LANES), jnp.float32),
            pltpu.SemaphoreType.DMA((s,)),
            pltpu.SemaphoreType.DMA((s,)),
            pltpu.SemaphoreType.DMA((s,)),
            *scratch,
        ],
        cost_estimate=pl.CostEstimate(
            flops=flops,
            bytes_accessed=4 * plan.all_rows * own * width + 2 * width * width,
            transcendentals=0,
        ),
        name="sections",
    )(*pieces, *gathered, left)


def load_piece(plan, piece, mixed, sem):
    for r in range(plan.out_rows):
        for m in range(plan.seq * plan.ch):
            row = (m % plan.ch) * plan.chunk + (m // plan.ch) * plan.own
            pltpu.make_async_copy(
                piece.at[m, r], mixed.at[r, pl.ds(row, plan.own)], sem.at[r]
            ).start()


def load_halves(plan, block, pieces, mixed, sem):
    me, y = lax.axis_index("seq"), lax.axis_index("ch")
    half, own = plan.half, plan.own
    for r in range(plan.out_rows):
        for m in range(half * plan.ch):
            row = (m % plan.ch) * plan.chunk + ((me // half) * half + m // plan.ch) * own
            pltpu.make_async_copy(
                block.at[m, r], mixed.at[r, pl.ds(pl.multiple_of(row, own), own)], sem.at[r]
            ).start()
            who = jnp.bitwise_xor(me, half + m // plan.ch)
            row = jnp.bitwise_xor(y, m % plan.ch) * plan.chunk + who * own
            pltpu.make_async_copy(
                pieces[m].at[r], mixed.at[r, pl.ds(pl.multiple_of(row, own), own)], sem.at[r]
            ).start()


def load_shares(plan, shares, inputs, sem):
    y = lax.axis_index("ch")
    for r in range(plan.out_rows):
        for n in range(plan.ch):
            at = pl.ds(jnp.bitwise_xor(y, n) * plan.chunk, plan.chunk)
            pltpu.make_async_copy(shares[n].at[r], inputs.at[r, at], sem.at[r]).start()


def wait_row(buffer, sem, r):
    pltpu.make_async_copy(buffer.at[r], buffer.at[r], sem.at[r]).wait()


def column(plan, chunk, j):
    row = j * plan.mix
    return (row // plan.chunk) * plan.local + chunk * plan.chunk + row % plan.chunk


def silu(value):
    return value / (1.0 + jnp.exp(-value))


def turn_dot(value, weight):
    return lax.dot_general(
        value, weight, (((0,), (0,)), ((), ())), preferred_element_type=jnp.float32
    )


def gate_kernel(plan, *refs):
    c = plan.ch
    count = 1 + plan.half * c
    block, pieces, refs = refs[0], refs[1:count], refs[count:]
    shares, later = refs[:c], refs[c : 2 * c]
    gain, weight, out, gates, totals = refs[2 * c : 5 + 2 * c]
    mixed, inputs, after, sem_m, sem_i, sem_a = refs[5 + 2 * c :]
    i = pl.program_id(0)

    @pl.when(i == 0)
    def _():
        load_shares(plan, later, after, sem_a)
        load_shares(plan, shares, inputs, sem_i)
        load_halves(plan, block, pieces, mixed, sem_m)

    wait_row(after, sem_a, i)
    wait_row(inputs, sem_i, i)
    wait_row(mixed, sem_m, i)

    def tile(kt, carry):
        ks = pl.ds(pl.multiple_of(kt * LANES, LANES), LANES)
        total = jnp.zeros((1, LANES), jnp.float32)
        for j in range(plan.chunk * c // plan.mix):
            rs = pl.ds(j * plan.mix, plan.mix)
            gates[0, rs, ks] = silu(after[i, rs, ks].astype(jnp.float32)).astype(jnp.bfloat16)
            value = mixed[i, rs, ks].astype(jnp.float32)
            value = value * silu(inputs[i, rs, ks].astype(jnp.float32))
            value = value.astype(jnp.bfloat16).astype(jnp.float32)
            total = total + jnp.sum(value * value, axis=0, keepdims=True)
            col = column(plan, 0, j)
            value = (value * gain[pl.ds(col, plan.mix), :]).astype(jnp.bfloat16)
            out[ks, rs] = turn_dot(value, weight[col // plan.mix]).astype(jnp.bfloat16)
        totals[0, :, ks] = jnp.broadcast_to(total, (8, LANES))
        return carry

    lax.fori_loop(0, plan.width // LANES, tile, 0)


def final_kernel(plan, *refs):
    piece, gates, held, before, gain, weight, result = refs[:7]
    mixed, inputs, left, out, sem_m, sem_i, sem_h, sem_o = refs[7:]
    c, width = plan.ch, plan.width
    for r in range(plan.out_rows):
        pltpu.make_async_copy(gates.at[r], inputs.at[r], sem_i.at[r]).start()
        at = pl.ds(r * width, width)
        pltpu.make_async_copy(held.at[at], left.at[r], sem_h.at[r]).start()
    load_piece(plan, piece, mixed, sem_m)
    stores = []
    for r in range(plan.out_rows):
        wait_row(mixed, sem_m, r)
        wait_row(inputs, sem_i, r)
        wait_row(left, sem_h, r)

        def tile(kt, carry):
            ks = pl.ds(pl.multiple_of(kt * LANES, LANES), LANES)
            total = before[r, pl.ds(0, 1), ks]
            parts = []
            for j in range(plan.chunk * c // plan.mix):
                rs = pl.ds(j * plan.mix, plan.mix)
                value = mixed[r, rs, ks].astype(jnp.float32)
                value = value * inputs[r, rs, ks].astype(jnp.float32)
                total = total + jnp.sum(value * value, axis=0, keepdims=True)
                col = column(plan, 1, j)
                value = (value * gain[pl.ds(col, plan.mix), :]).astype(jnp.bfloat16)
                parts.append((col, turn_dot(value, weight[col // plan.mix])))
            inverse = lax.rsqrt(total * (1.0 / plan.channels) + 1e-05)
            scale = jnp.broadcast_to(inverse, (128, LANES)).T
            for col, part in parts:
                for q in range(plan.mix // 128):
                    value = part[:, q * 128 : (q + 1) * 128] * scale
                    out[r, ks, pl.ds(col + q * 128, 128)] = value.astype(jnp.bfloat16)
            for j in range(plan.chunk * c // 128):
                value = left[r, ks, pl.ds(j * 128, 128)].astype(jnp.float32) * scale
                col = (j * 128 // plan.chunk) * plan.local + j * 128 % plan.chunk
                out[r, ks, pl.ds(col, 128)] = value.astype(jnp.bfloat16)
            return carry

        lax.fori_loop(0, width // LANES, tile, 0)
        stores.append(
            pltpu.make_async_copy(out.at[r], result.at[pl.ds(r * width, width)], sem_o.at[r])
        )
        stores[-1].start()
    for store in stores:
        store.wait()


def gate(plan, pieces, shares, later, gain, weight):
    size, part = plan.out_rows * plan.width, plan.chunk * plan.ch
    shape, bf16 = (plan.out_rows, part, plan.width), jnp.bfloat16
    sem = pltpu.SemaphoreType.DMA((plan.out_rows,))
    return pl.pallas_call(
        functools.partial(gate_kernel, plan),
        out_shape=[
            jax.ShapeDtypeStruct((size, part), bf16),
            jax.ShapeDtypeStruct(shape, bf16),
            jax.ShapeDtypeStruct((plan.out_rows, 8, plan.width), jnp.float32),
        ],
        grid=(plan.out_rows,),
        in_specs=[ANY] * (len(pieces) + 2 * plan.ch) + [VMEM, VMEM],
        out_specs=[
            pl.BlockSpec((plan.width, part), lambda i: (i, 0)),
            pl.BlockSpec((1, part, plan.width), lambda i: (i, 0, 0)),
            pl.BlockSpec((1, 8, plan.width), lambda i: (i, 0, 0)),
        ],
        scratch_shapes=[pltpu.VMEM(shape, bf16)] * 3 + [sem] * 3,
        cost_estimate=pl.CostEstimate(
            flops=2 * size * part * plan.mix,
            bytes_accessed=10 * size * part,
            transcendentals=2 * size * part,
        ),
        name="gate",
    )(*pieces, *shares, *later, gain, weight)


def final(plan, piece, gates, held, before, gain, weight):
    size, part = plan.out_rows * plan.width, plan.chunk * plan.ch
    shape, bf16 = (plan.out_rows, part, plan.width), jnp.bfloat16
    sem = pltpu.SemaphoreType.DMA((plan.out_rows,))
    return pl.pallas_call(
        functools.partial(final_kernel, plan),
        out_shape=jax.ShapeDtypeStruct((size, plan.channels), bf16),
        in_specs=[ANY] * 3 + [VMEM] * 3,
        out_specs=ANY,
        scratch_shapes=[
            pltpu.VMEM(shape, bf16),
            pltpu.VMEM(shape, bf16),
            pltpu.VMEM((plan.out_rows, plan.width, part), bf16),
            pltpu.VMEM((plan.out_rows, plan.width, plan.channels), bf16),
        ]
        + [sem] * 4,
        cost_estimate=pl.CostEstimate(
            flops=2 * size * part * plan.mix,
            bytes_accessed=10 * size * part,
            transcendentals=0,
        ),
        name="final",
    )(piece, gates, held, before, gain, weight)


def swap(value, mask, axis):
    count = lax.axis_size(axis)
    return lax.ppermute(value, axis, [(i, i ^ mask) for i in range(count)])


def exchange(value, axes):
    return lax.all_to_all(value, axes, split_axis=0, concat_axis=0, tiled=True)


def chunked_body(plan, tokens, right_block, twiddle, left_block, gain, mix_weight):
    s, c, near, own = plan.seq, plan.ch, plan.near, plan.own
    pad = plan.gather_rows - right_block.shape[0] - twiddle.shape[0]
    zeros = jnp.zeros((pad, plan.width), jnp.bfloat16)
    held = jnp.concatenate([right_block, twiddle, zeros], axis=0)[None]
    gain = jnp.broadcast_to(gain[:, None], (plan.channels, LANES))
    column = [held]
    for n in range(1, s // near):
        column.append(swap(held, n * near, "seq"))
    column = jnp.concatenate(column, axis=0)
    gathered = [column]
    for m in range(1, near):
        gathered.append(swap(column, m, "seq"))
    arrived, shares = [], []
    for k in range(CHUNKS):
        pieces, share = prep(plan, tokens, k, k == 1)
        if k == 0:
            block = exchange(pieces, "seq")
            arrived.append([block.reshape(plan.all_rows, own, plan.width)])
        else:
            arrived.append([pieces[0]] + [None] * (s - 1))
            for m in reversed(range(1, s)):
                arrived[k][m] = swap(pieces[m], m, "seq")
        shares.append([share[0]])
        for n in range(1, c):
            shares[k].append(swap(share[n], n, "ch"))
    half = plan.half
    block, *pieces = sections(plan, arrived[0], gathered, left_block, True)
    block = block.reshape(half * c, plan.out_rows, own, plan.width)
    groups = [[h * half * c + i for i in range(half * c)] for h in range(2)]
    landed = [
        lax.all_to_all(
            block, ("seq", "ch"), 0, 0, axis_index_groups=groups, tiled=True
        )
    ]
    for m in range(half):
        for n in range(c):
            landed.append(cross(pieces[m * c + n], half + m, n, s, c))
    out = sections(plan, arrived[1], gathered, left_block, False)
    out = out.reshape(s * c, plan.out_rows, own, plan.width)
    last = exchange(out, ("seq", "ch"))
    held, gates, before = gate(plan, landed, *shares, gain, mix_weight)
    return final(plan, last, gates, held, before, gain, mix_weight)


def cross(value, seq_mask, ch_mask, s, c):
    pairs = [(i * c + j, (i ^ seq_mask) * c + (j ^ ch_mask)) for i in range(s) for j in range(c)]
    return lax.ppermute(value, ("seq", "ch"), pairs)


def plain_body(tokens, right_block, twiddle, left_block, gain, mix_weight):
    row_width = right_block.shape[1]
    row_count = tokens.shape[0] // row_width
    local_width = tokens.shape[1]
    inputs = tokens.reshape(row_count, row_width, local_width)
    whole_right = lax.all_gather(right_block, "seq", axis=0, tiled=True)
    first_section = jnp.einsum(
        "abc,bk->akc", inputs, whole_right, preferred_element_type=jnp.float32
    )
    spread = (first_section * twiddle.astype(jnp.float32)[:, :, None]).astype(jnp.bfloat16)
    mixed_rows = jnp.einsum(
        "ij,jbc->ibc",
        left_block,
        lax.all_to_all(spread, "seq", split_axis=1, concat_axis=0, tiled=True),
        preferred_element_type=jnp.float32,
    ).astype(jnp.bfloat16)
    sequence_mixed = lax.all_to_all(mixed_rows, "seq", split_axis=0, concat_axis=1, tiled=True)
    gated = (sequence_mixed.astype(jnp.float32) * jax.nn.silu(inputs.astype(jnp.float32))).astype(
        jnp.bfloat16
    )
    ch_count = lax.axis_size("ch")
    pieces = gated.reshape(ch_count, row_count * row_width // ch_count, local_width)
    shard_piece = lax.all_to_all(pieces, "ch", split_axis=0, concat_axis=2, tiled=True)
    values = shard_piece.astype(jnp.float32)
    inverse_rms = lax.rsqrt(jnp.mean(values * values, axis=-1, keepdims=True) + 1e-05)
    normed = (values * inverse_rms * gain).astype(jnp.bfloat16)
    block_count = mix_weight.shape[0]
    block_width = mix_weight.shape[1]
    normed = normed.reshape(shard_piece.shape[0], shard_piece.shape[1], block_count, block_width)
    result = jnp.einsum("otki,kij->otkj", normed, mix_weight, preferred_element_type=jnp.float32)
    mixed_out = result.astype(jnp.bfloat16).reshape(shard_piece.shape)
    return mixed_out.reshape(mixed_out.shape[1], mixed_out.shape[2])


def body(tokens, right_block, twiddle, left_block, gain, mix_weight):
    plan = Plan(tokens, right_block, twiddle, left_block, mix_weight)
    if plan.fits():
        return chunked_body(plan, tokens, right_block, twiddle, left_block, gain, mix_weight)
    return plain_body(tokens, right_block, twiddle, left_block, gain, mix_weight)


def solution(mesh):
    in_specs = (P("seq", "ch"), P("seq", None), P("seq", None), P(), P(), P())
    out_specs = P(("seq", "ch"), None)
    return jax.shard_map(body, mesh=mesh, in_specs=in_specs, out_specs=out_specs, check_vma=False)
```

```python
import functools

import jax
import jax.numpy as jnp
from jax import lax
from jax.experimental import pallas as pl
from jax.experimental.pallas import tpu as pltpu
from jax.sharding import PartitionSpec as P


ANY = pl.BlockSpec(memory_space=pl.ANY)
VMEM = pl.BlockSpec(memory_space=pltpu.VMEM)
LANES = 256
CHUNKS = 2
STEP = 16
LAST = 1


class Plan:
    def __init__(self, tokens, right_block, twiddle, left_block, mix_weight):
        self.seq = lax.axis_size("seq")
        self.ch = lax.axis_size("ch")
        self.width = right_block.shape[1]
        self.rows = tokens.shape[0] // self.width
        self.local = tokens.shape[1]
        self.right_rows = right_block.shape[0]
        self.all_rows = left_block.shape[0]
        self.chunk = self.local // CHUNKS
        self.own = self.chunk // self.seq
        self.out_rows = self.rows // self.ch
        self.channels = self.local * self.ch
        self.mix = mix_weight.shape[1]
        self.half = self.seq // 2
        self.near = 1
        while self.near * self.near < self.seq:
            self.near *= 2
        pad = self.right_rows + twiddle.shape[0]
        self.gather_rows = pad + (-pad) % 16

    def fits(self):
        s, c = self.seq, self.ch
        return (
            s > 1
            and s <= 16
            and c > 1
            and c <= 4
            and s & (s - 1) == 0
            and c & (c - 1) == 0
            and self.own % 16 == 0
            and self.own > 0
            and self.chunk % 128 == 0
            and self.rows % 8 == 0
            and STEP % self.rows == 0
            and self.rows % c == 0
            and self.out_rows > LAST
            and self.all_rows % STEP == 0
            and self.right_rows % 16 == 0
            and self.width % LANES == 0
            and self.mix % 128 == 0
            and self.chunk % self.mix == 0
        )


def prep_kernel(plan, chunk, split, x_ref, *rest):
    s = plan.seq
    count = s if split else 1
    outs, shares = rest[:count], rest[count:-5]
    given, turned, in_sem, out_sem, share_sem = rest[-5:]
    me, y = lax.axis_index("seq"), lax.axis_index("ch")
    loads = [
        pltpu.make_async_copy(
            x_ref.at[pl.ds(a * plan.width, plan.width), pl.ds(chunk * plan.chunk, plan.chunk)],
            given.at[a],
            in_sem.at[a],
        )
        for a in range(plan.rows)
    ]
    for load in loads:
        load.start()
    stores = []
    for a in range(plan.rows):
        loads[a].wait()
        turned[a] = given[a].T.reshape(s, plan.own, plan.width)
        if split:
            for m in range(s):
                pltpu.make_async_copy(
                    turned.at[a, jnp.bitwise_xor(me, m)], outs[m].at[a], out_sem.at[m]
                ).start()
        else:
            stores.append(
                pltpu.make_async_copy(turned.at[a], outs[0].at[:, a], out_sem.at[a])
            )
            stores[-1].start()
    for m in range(len(shares)):
        at = pl.ds(jnp.bitwise_xor(y, m) * plan.out_rows, plan.out_rows)
        stores.append(pltpu.make_async_copy(turned.at[at], shares[m], share_sem.at[m]))
        stores[-1].start()
    if split:
        for m in range(s):
            pltpu.make_async_copy(
                turned.at[:, jnp.bitwise_xor(me, m)], outs[m], out_sem.at[m]
            ).wait()
    for store in stores:
        store.wait()


def prep(plan, tokens, chunk, split):
    bf16 = jnp.bfloat16
    if split:
        shapes = [jax.ShapeDtypeStruct((plan.rows, plan.own, plan.width), bf16)] * plan.seq
        shape = (plan.out_rows, plan.seq, plan.own, plan.width)
        shapes += [jax.ShapeDtypeStruct(shape, bf16)] * plan.ch
    else:
        shape = (plan.seq, plan.rows, plan.own, plan.width)
        shapes = [jax.ShapeDtypeStruct(shape, bf16)]
    out = pl.pallas_call(
        functools.partial(prep_kernel, plan, chunk, split),
        out_shape=shapes,
        in_specs=[ANY],
        out_specs=[ANY] * len(shapes),
        scratch_shapes=[
            pltpu.VMEM((plan.rows, plan.width, plan.chunk), bf16),
            pltpu.VMEM((plan.rows, plan.seq, plan.own, plan.width), bf16),
            pltpu.SemaphoreType.DMA((plan.rows,)),
            pltpu.SemaphoreType.DMA((max(plan.seq, plan.rows),)),
            pltpu.SemaphoreType.DMA((plan.ch,)),
        ],
        cost_estimate=pl.CostEstimate(
            flops=0,
            bytes_accessed=6 * plan.rows * plan.chunk * plan.width,
            transcendentals=0,
        ),
        name="prep",
    )(tokens)
    if split:
        shape = (plan.out_rows, plan.chunk, plan.width)
        return out[: plan.seq], [share.reshape(shape) for share in out[plan.seq :]]
    return out[0], [own_rows(plan, out[0], n) for n in range(plan.ch)]


def own_rows(plan, block, mask):
    start = jnp.bitwise_xor(lax.axis_index("ch"), mask) * plan.out_rows
    part = lax.dynamic_slice_in_dim(block, start, plan.out_rows, axis=1)
    return part.transpose(1, 0, 2, 3).reshape(plan.out_rows, plan.chunk, plan.width)


def sections_kernel(plan, count, full, *refs):
    near, far, own = plan.near, plan.seq // plan.near, plan.own
    pieces, gathered, left = refs[:count], refs[count : count + near], refs[count + near]
    parts = 1 + plan.half * plan.ch * (2 if full else 1)
    outs = refs[count + near + 1 : count + near + 1 + parts]
    x, right, twiddle, first, mixed, out = refs[count + near + 1 + parts : -5]
    sem_x, sem_r, sem_t, sem_o, sem_l = refs[-5:]
    me, y = lax.axis_index("seq"), lax.axis_index("ch")
    if count == 1:
        copies = [pltpu.make_async_copy(pieces[0], x, sem_x.at[0])]
    else:
        copies = [
            pltpu.make_async_copy(
                pieces[m], x.at[pl.ds(jnp.bitwise_xor(me, m) * plan.rows, plan.rows)], sem_x.at[m]
            )
            for m in range(count)
        ]
    for m in range(near):
        for n in range(far):
            who = jnp.bitwise_xor(me, n * near + m)
            at = pl.ds(pl.multiple_of(who * plan.right_rows, plan.right_rows), plan.right_rows)
            source = gathered[m].at[n]
            copies.append(
                pltpu.make_async_copy(
                    source.at[pl.ds(0, plan.right_rows)], right.at[at], sem_r.at[m * far + n]
                )
            )
            copies.append(
                pltpu.make_async_copy(
                    source.at[pl.ds(plan.right_rows, plan.rows)],
                    twiddle.at[who],
                    sem_t.at[m * far + n],
                )
            )
    kt = pl.program_id(0)

    @pl.when(kt == 0)
    def _():
        for copy in copies:
            copy.start()
        for copy in copies:
            copy.wait()

    ks = pl.ds(pl.multiple_of(kt * LANES, LANES), LANES)

    def section_one(t, carry):
        rows = x[pl.ds(t * STEP, STEP)].reshape(STEP * own, plan.width)
        value = jnp.dot(rows, right[:, ks], preferred_element_type=jnp.float32)
        value = value.reshape(STEP, own, LANES)
        group = STEP // plan.rows
        factor = twiddle[pl.ds(t * group, group), :, ks].astype(jnp.float32)
        value = value * factor.reshape(STEP, LANES)[:, None, :]
        at = pl.ds(pl.multiple_of(t * STEP, STEP), STEP)
        first[:, at, :] = jnp.swapaxes(value, 0, 1).astype(jnp.bfloat16)
        return carry

    lax.fori_loop(0, plan.all_rows // STEP, section_one, 0)
    for q in range(own):
        mixed[q] = jnp.dot(left[...], first[q], preferred_element_type=jnp.float32)

    def turn(t, carry):
        at = pl.ds(pl.multiple_of(t * STEP, STEP), STEP)
        value = jnp.swapaxes(mixed[:, at, :], 0, 1)
        out[pl.ds(t * STEP, STEP), :, ks] = value.astype(jnp.bfloat16)
        return carry

    lax.fori_loop(0, plan.all_rows // STEP, turn, 0)

    @pl.when(kt == plan.width // LANES - 1)
    def _():
        half, ways, rows = plan.half, plan.half * plan.ch, plan.out_rows
        stores = []
        low = 0 if full else half
        for m in range((plan.seq - low) * plan.ch):
            row = jnp.bitwise_xor(me, low + m // plan.ch) * plan.rows
            row = row + jnp.bitwise_xor(y, m % plan.ch) * rows
            at = pl.ds(row + full, rows - full)
            stores.append(pltpu.make_async_copy(out.at[at], outs[1 + m], sem_o.at[m]))
        for m in range(2 * ways if full else ways):
            row = m * rows if full else (me // half) * (half * plan.rows) + m * rows
            at = pl.ds(row, full if full else rows)
            stores.append(pltpu.make_async_copy(out.at[at], outs[0].at[m], sem_l.at[m]))
        for store in stores:
            store.start()
        for store in stores:
            store.wait()


def sections(plan, pieces, gathered, left, full):
    s, own, width, bf16 = plan.seq, plan.own, plan.width, jnp.bfloat16
    flops = 2 * plan.all_rows * own * width * (width + plan.all_rows)
    ways = plan.half * plan.ch
    count = 2 * ways if full else ways
    shapes = [jax.ShapeDtypeStruct((count, full if full else plan.out_rows, own, width), bf16)]
    shapes += [jax.ShapeDtypeStruct((plan.out_rows - full, own, width), bf16)] * count
    return pl.pallas_call(
        functools.partial(sections_kernel, plan, len(pieces), full),
        out_shape=shapes,
        grid=(width // LANES,),
        in_specs=[ANY] * (len(pieces) + len(gathered)) + [VMEM],
        out_specs=[ANY] * len(shapes),
        scratch_shapes=[
            pltpu.VMEM((plan.all_rows, own, width), bf16),
            pltpu.VMEM((s * plan.right_rows, width), bf16),
            pltpu.VMEM((s, plan.rows, width), bf16),
            pltpu.VMEM((own, plan.all_rows, LANES), bf16),
            pltpu.VMEM((own, plan.all_rows, LANES), jnp.float32),
            pltpu.VMEM((plan.all_rows, own, width), bf16),
            pltpu.SemaphoreType.DMA((s,)),
            pltpu.SemaphoreType.DMA((s,)),
            pltpu.SemaphoreType.DMA((s,)),
            pltpu.SemaphoreType.DMA((2 * ways,)),
            pltpu.SemaphoreType.DMA((2 * ways,)),
        ],
        cost_estimate=pl.CostEstimate(
            flops=flops,
            bytes_accessed=4 * plan.all_rows * own * width + 2 * width * width,
            transcendentals=0,
        ),
        name="sections",
    )(*pieces, *gathered, left)


def load_piece(plan, piece, mixed, sem):
    for r in range(piece.shape[1]):
        for m in range(plan.seq * plan.ch):
            row = (m % plan.ch) * plan.chunk + (m // plan.ch) * plan.own
            pltpu.make_async_copy(
                piece.at[m, r], mixed.at[r, pl.ds(row, plan.own)], sem.at[r]
            ).start()


def load_halves(plan, block, pieces, mixed, sem):
    me, y = lax.axis_index("seq"), lax.axis_index("ch")
    half, own = plan.half, plan.own
    for r in range(block.shape[1]):
        for m in range(half * plan.ch):
            row = (m % plan.ch) * plan.chunk + ((me // half) * half + m // plan.ch) * own
            pltpu.make_async_copy(
                block.at[m, r], mixed.at[r, pl.ds(pl.multiple_of(row, own), own)], sem.at[r]
            ).start()
            who = jnp.bitwise_xor(me, half + m // plan.ch)
            row = jnp.bitwise_xor(y, m % plan.ch) * plan.chunk + who * own
            pltpu.make_async_copy(
                pieces[m].at[r], mixed.at[r, pl.ds(pl.multiple_of(row, own), own)], sem.at[r]
            ).start()


def load_pieces(plan, pieces, mixed, sem):
    me, y = lax.axis_index("seq"), lax.axis_index("ch")
    for r in range(pieces[0].shape[0]):
        for m, piece in enumerate(pieces):
            row = jnp.bitwise_xor(y, m % plan.ch) * plan.chunk
            row = row + jnp.bitwise_xor(me, m // plan.ch) * plan.own
            at = pl.ds(pl.multiple_of(row, plan.own), plan.own)
            pltpu.make_async_copy(piece.at[r], mixed.at[r, at], sem.at[r]).start()


def load_shares(plan, shares, inputs, sem):
    y = lax.axis_index("ch")
    for r in range(plan.out_rows):
        for n in range(plan.ch):
            at = pl.ds(jnp.bitwise_xor(y, n) * plan.chunk, plan.chunk)
            pltpu.make_async_copy(shares[n].at[r], inputs.at[r, at], sem.at[r]).start()


def wait_row(buffer, sem, r):
    pltpu.make_async_copy(buffer.at[r], buffer.at[r], sem.at[r]).wait()


def column(plan, chunk, j):
    row = j * plan.mix
    return (row // plan.chunk) * plan.local + chunk * plan.chunk + row % plan.chunk


def silu(value):
    return value / (1.0 + jnp.exp(-value))


def turn_dot(value, weight):
    return lax.dot_general(
        value, weight, (((0,), (0,)), ((), ())), preferred_element_type=jnp.float32
    )


def gate_kernel(plan, *refs):
    c = plan.ch
    count = 1 + plan.half * c
    block, pieces, refs = refs[0], refs[1:count], refs[count:]
    shares, later = refs[:c], refs[c : 2 * c]
    gain, weight, out, gates, totals = refs[2 * c : 5 + 2 * c]
    mixed, inputs, after, sem_m, sem_i, sem_a = refs[5 + 2 * c :]
    i = pl.program_id(0)

    @pl.when(i == 0)
    def _():
        load_shares(plan, later, after, sem_a)
        load_shares(plan, shares, inputs, sem_i)
        load_halves(plan, block, pieces, mixed, sem_m)

    wait_row(after, sem_a, i)
    wait_row(inputs, sem_i, i)
    wait_row(mixed, sem_m, i)

    def tile(kt, carry):
        ks = pl.ds(pl.multiple_of(kt * LANES, LANES), LANES)
        total = jnp.zeros((1, LANES), jnp.float32)
        for j in range(plan.chunk * c // plan.mix):
            rs = pl.ds(j * plan.mix, plan.mix)
            gates[0, rs, ks] = silu(after[i, rs, ks].astype(jnp.float32)).astype(jnp.bfloat16)
            value = mixed[i, rs, ks].astype(jnp.float32)
            value = value * silu(inputs[i, rs, ks].astype(jnp.float32))
            value = value.astype(jnp.bfloat16).astype(jnp.float32)
            total = total + jnp.sum(value * value, axis=0, keepdims=True)
            col = column(plan, 0, j)
            value = (value * gain[pl.ds(col, plan.mix), :]).astype(jnp.bfloat16)
            out[ks, rs] = turn_dot(value, weight[col // plan.mix]).astype(jnp.bfloat16)
        totals[0, :, ks] = jnp.broadcast_to(total, (8, LANES))
        return carry

    lax.fori_loop(0, plan.width // LANES, tile, 0)


def final_kernel(plan, count, base, rows, *refs):
    pieces, gates, held, before, gain, weight = refs[:count], *refs[count : count + 5]
    result = refs[-9]
    mixed, inputs, left, out, sem_m, sem_i, sem_h, sem_o = refs[-8:]
    c, width = plan.ch, plan.width
    for r in range(rows):
        pltpu.make_async_copy(gates.at[base + r], inputs.at[r], sem_i.at[r]).start()
        at = pl.ds((base + r) * width, width)
        pltpu.make_async_copy(held.at[at], left.at[r], sem_h.at[r]).start()
    if count == 1:
        load_piece(plan, pieces[0], mixed, sem_m)
    else:
        load_pieces(plan, pieces, mixed, sem_m)
    stores = []
    for r in range(rows):
        wait_row(mixed, sem_m, r)
        wait_row(inputs, sem_i, r)
        wait_row(left, sem_h, r)

        def tile(kt, carry):
            ks = pl.ds(pl.multiple_of(kt * LANES, LANES), LANES)
            total = before[base + r, pl.ds(0, 1), ks]
            parts = []
            for j in range(plan.chunk * c // plan.mix):
                rs = pl.ds(j * plan.mix, plan.mix)
                value = mixed[r, rs, ks].astype(jnp.float32)
                value = value * inputs[r, rs, ks].astype(jnp.float32)
                total = total + jnp.sum(value * value, axis=0, keepdims=True)
                col = column(plan, 1, j)
                value = (value * gain[pl.ds(col, plan.mix), :]).astype(jnp.bfloat16)
                parts.append((col, turn_dot(value, weight[col // plan.mix])))
            inverse = lax.rsqrt(total * (1.0 / plan.channels) + 1e-05)
            scale = jnp.broadcast_to(inverse, (128, LANES)).T
            for col, part in parts:
                for q in range(plan.mix // 128):
                    value = part[:, q * 128 : (q + 1) * 128] * scale
                    out[r, ks, pl.ds(col + q * 128, 128)] = value.astype(jnp.bfloat16)
            for j in range(plan.chunk * c // 128):
                value = left[r, ks, pl.ds(j * 128, 128)].astype(jnp.float32) * scale
                col = (j * 128 // plan.chunk) * plan.local + j * 128 % plan.chunk
                out[r, ks, pl.ds(col, 128)] = value.astype(jnp.bfloat16)
            return carry

        lax.fori_loop(0, width // LANES, tile, 0)
        stores.append(
            pltpu.make_async_copy(out.at[r], result.at[pl.ds((base + r) * width, width)], sem_o.at[r])
        )
        stores[-1].start()
    for store in stores:
        store.wait()


def gate(plan, pieces, shares, later, gain, weight):
    size, part = plan.out_rows * plan.width, plan.chunk * plan.ch
    shape, bf16 = (plan.out_rows, part, plan.width), jnp.bfloat16
    sem = pltpu.SemaphoreType.DMA((plan.out_rows,))
    return pl.pallas_call(
        functools.partial(gate_kernel, plan),
        out_shape=[
            jax.ShapeDtypeStruct((size, part), bf16),
            jax.ShapeDtypeStruct(shape, bf16),
            jax.ShapeDtypeStruct((plan.out_rows, 8, plan.width), jnp.float32),
        ],
        grid=(plan.out_rows,),
        in_specs=[ANY] * (len(pieces) + 2 * plan.ch) + [VMEM, VMEM],
        out_specs=[
            pl.BlockSpec((plan.width, part), lambda i: (i, 0)),
            pl.BlockSpec((1, part, plan.width), lambda i: (i, 0, 0)),
            pl.BlockSpec((1, 8, plan.width), lambda i: (i, 0, 0)),
        ],
        scratch_shapes=[pltpu.VMEM(shape, bf16)] * 3 + [sem] * 3,
        cost_estimate=pl.CostEstimate(
            flops=2 * size * part * plan.mix,
            bytes_accessed=10 * size * part,
            transcendentals=2 * size * part,
        ),
        name="gate",
    )(*pieces, *shares, *later, gain, weight)


def final(plan, pieces, gates, held, before, gain, weight, base, rows, result=None):
    size, part = rows * plan.width, plan.chunk * plan.ch
    shape, bf16 = (rows, part, plan.width), jnp.bfloat16
    sem = pltpu.SemaphoreType.DMA((rows,))
    args = [*pieces, gates, held, before, gain, weight]
    aliases = {}
    if result is not None:
        aliases[len(args)] = 0
        args.append(result)
    return pl.pallas_call(
        functools.partial(final_kernel, plan, len(pieces), base, rows),
        out_shape=jax.ShapeDtypeStruct((plan.out_rows * plan.width, plan.channels), bf16),
        in_specs=[ANY] * (len(pieces) + 2) + [VMEM] * 3 + [ANY] * len(aliases),
        out_specs=ANY,
        input_output_aliases=aliases,
        scratch_shapes=[
            pltpu.VMEM(shape, bf16),
            pltpu.VMEM(shape, bf16),
            pltpu.VMEM((rows, plan.width, part), bf16),
            pltpu.VMEM((rows, plan.width, plan.channels), bf16),
        ]
        + [sem] * 4,
        cost_estimate=pl.CostEstimate(
            flops=2 * size * part * plan.mix,
            bytes_accessed=10 * size * part,
            transcendentals=0,
        ),
        name="final",
    )(*args)


def swap(value, mask, axis):
    count = lax.axis_size(axis)
    return lax.ppermute(value, axis, [(i, i ^ mask) for i in range(count)])


def exchange(value, axes):
    return lax.all_to_all(value, axes, split_axis=0, concat_axis=0, tiled=True)


def chunked_body(plan, tokens, right_block, twiddle, left_block, gain, mix_weight):
    s, c, near, own = plan.seq, plan.ch, plan.near, plan.own
    pad = plan.gather_rows - right_block.shape[0] - twiddle.shape[0]
    zeros = jnp.zeros((pad, plan.width), jnp.bfloat16)
    held = jnp.concatenate([right_block, twiddle, zeros], axis=0)[None]
    gain = jnp.broadcast_to(gain[:, None], (plan.channels, LANES))
    column = [held]
    for n in range(1, s // near):
        column.append(swap(held, n * near, "seq"))
    column = jnp.concatenate(column, axis=0)
    gathered = [column]
    for m in range(1, near):
        gathered.append(swap(column, m, "seq"))
    arrived, shares = [], []
    for k in range(CHUNKS):
        pieces, share = prep(plan, tokens, k, k == 1)
        if k == 0:
            block = exchange(pieces, "seq")
            arrived.append([block.reshape(plan.all_rows, own, plan.width)])
        else:
            arrived.append([pieces[0]] + [None] * (s - 1))
            for m in reversed(range(1, s)):
                arrived[k][m] = swap(pieces[m], m, "seq")
        shares.append([share[0]])
        for n in range(1, c):
            shares[k].append(swap(share[n], n, "ch"))
    half, ways = plan.half, plan.half * c
    groups = [[h * ways + i for i in range(ways)] for h in range(2)]
    first = plan.out_rows - LAST
    landed = []
    for k in range(CHUNKS):
        block, *pieces = sections(plan, arrived[k], gathered, left_block, k * first)
        low = 0 if k else half
        if k:
            block = exchange(block, ("seq", "ch"))
        else:
            block = lax.all_to_all(block, ("seq", "ch"), 0, 0, axis_index_groups=groups, tiled=True)
        landed.append([block])
        for m in range(low, s):
            for n in range(c):
                piece = pieces[(m - low) * c + n]
                if m or n:
                    piece = cross(piece, m, n, s, c)
                landed[k].append(piece)
    held, gates, before = gate(plan, landed[0], *shares, gain, mix_weight)
    rest = (gates, held, before, gain, mix_weight)
    result = final(plan, landed[1][:1], *rest, 0, first)
    return final(plan, landed[1][1:], *rest, first, LAST, result)


def cross(value, seq_mask, ch_mask, s, c):
    pairs = [(i * c + j, (i ^ seq_mask) * c + (j ^ ch_mask)) for i in range(s) for j in range(c)]
    return lax.ppermute(value, ("seq", "ch"), pairs)


def plain_body(tokens, right_block, twiddle, left_block, gain, mix_weight):
    row_width = right_block.shape[1]
    row_count = tokens.shape[0] // row_width
    local_width = tokens.shape[1]
    inputs = tokens.reshape(row_count, row_width, local_width)
    whole_right = lax.all_gather(right_block, "seq", axis=0, tiled=True)
    first_section = jnp.einsum(
        "abc,bk->akc", inputs, whole_right, preferred_element_type=jnp.float32
    )
    spread = (first_section * twiddle.astype(jnp.float32)[:, :, None]).astype(jnp.bfloat16)
    mixed_rows = jnp.einsum(
        "ij,jbc->ibc",
        left_block,
        lax.all_to_all(spread, "seq", split_axis=1, concat_axis=0, tiled=True),
        preferred_element_type=jnp.float32,
    ).astype(jnp.bfloat16)
    sequence_mixed = lax.all_to_all(mixed_rows, "seq", split_axis=0, concat_axis=1, tiled=True)
    gated = (sequence_mixed.astype(jnp.float32) * jax.nn.silu(inputs.astype(jnp.float32))).astype(
        jnp.bfloat16
    )
    ch_count = lax.axis_size("ch")
    pieces = gated.reshape(ch_count, row_count * row_width // ch_count, local_width)
    shard_piece = lax.all_to_all(pieces, "ch", split_axis=0, concat_axis=2, tiled=True)
    values = shard_piece.astype(jnp.float32)
    inverse_rms = lax.rsqrt(jnp.mean(values * values, axis=-1, keepdims=True) + 1e-05)
    normed = (values * inverse_rms * gain).astype(jnp.bfloat16)
    block_count = mix_weight.shape[0]
    block_width = mix_weight.shape[1]
    normed = normed.reshape(shard_piece.shape[0], shard_piece.shape[1], block_count, block_width)
    result = jnp.einsum("otki,kij->otkj", normed, mix_weight, preferred_element_type=jnp.float32)
    mixed_out = result.astype(jnp.bfloat16).reshape(shard_piece.shape)
    return mixed_out.reshape(mixed_out.shape[1], mixed_out.shape[2])


def body(tokens, right_block, twiddle, left_block, gain, mix_weight):
    plan = Plan(tokens, right_block, twiddle, left_block, mix_weight)
    if plan.fits():
        return chunked_body(plan, tokens, right_block, twiddle, left_block, gain, mix_weight)
    return plain_body(tokens, right_block, twiddle, left_block, gain, mix_weight)


def solution(mesh):
    in_specs = (P("seq", "ch"), P("seq", None), P("seq", None), P(), P(), P())
    out_specs = P(("seq", "ch"), None)
    return jax.shard_map(body, mesh=mesh, in_specs=in_specs, out_specs=out_specs, check_vma=False)
```

```python
import functools

import jax
import jax.numpy as jnp
from jax import lax
from jax.experimental import pallas as pl
from jax.experimental.pallas import tpu as pltpu
from jax.sharding import PartitionSpec as P


ANY = pl.BlockSpec(memory_space=pl.ANY)
VMEM = pl.BlockSpec(memory_space=pltpu.VMEM)
LANES = 256
CHUNKS = 2
STEP = 16
GRANT = 65472 * 1024
LAST = 1


class Plan:
    def __init__(self, tokens, right_block, twiddle, left_block, mix_weight):
        self.seq = lax.axis_size("seq")
        self.ch = lax.axis_size("ch")
        self.width = right_block.shape[1]
        self.rows = tokens.shape[0] // self.width
        self.local = tokens.shape[1]
        self.right_rows = right_block.shape[0]
        self.all_rows = left_block.shape[0]
        self.chunk = self.local // CHUNKS
        self.own = self.chunk // self.seq
        self.out_rows = self.rows // self.ch
        self.channels = self.local * self.ch
        self.mix = mix_weight.shape[1]
        self.half = self.seq // 2
        self.near = 1
        while self.near * self.near < self.seq:
            self.near *= 2
        pad = self.right_rows + twiddle.shape[0]
        self.gather_rows = pad + (-pad) % 8

    def fits(self):
        s, c = self.seq, self.ch
        return (
            s > 1
            and s <= 16
            and c > 1
            and c <= 4
            and s & (s - 1) == 0
            and c & (c - 1) == 0
            and self.own % 16 == 0
            and self.own > 0
            and self.chunk % 128 == 0
            and self.rows % 8 == 0
            and STEP % self.rows == 0
            and self.rows % c == 0
            and self.out_rows > LAST
            and self.all_rows % STEP == 0
            and self.right_rows % 16 == 0
            and self.width % LANES == 0
            and self.mix % 128 == 0
            and self.chunk % self.mix == 0
        )


def prep_kernel(plan, chunk, split, x_ref, *rest):
    s = plan.seq
    count = s if split else 1
    outs, shares = rest[:count], rest[count:-5]
    given, turned, in_sem, out_sem, share_sem = rest[-5:]
    me, y = lax.axis_index("seq"), lax.axis_index("ch")
    loads = [
        pltpu.make_async_copy(
            x_ref.at[pl.ds(a * plan.width, plan.width), pl.ds(chunk * plan.chunk, plan.chunk)],
            given.at[a],
            in_sem.at[a],
        )
        for a in range(plan.rows)
    ]
    for load in loads:
        load.start()
    stores = []
    for a in range(plan.rows):
        loads[a].wait()
        turned[a] = given[a].T.reshape(s, plan.own, plan.width)
        if split:
            for m in range(s):
                pltpu.make_async_copy(
                    turned.at[a, jnp.bitwise_xor(me, m)], outs[m].at[a], out_sem.at[m]
                ).start()
        else:
            stores.append(
                pltpu.make_async_copy(turned.at[a], outs[0].at[:, a], out_sem.at[a])
            )
            stores[-1].start()
    for m in range(len(shares)):
        at = pl.ds(jnp.bitwise_xor(y, m) * plan.out_rows, plan.out_rows)
        stores.append(pltpu.make_async_copy(turned.at[at], shares[m], share_sem.at[m]))
        stores[-1].start()
    if split:
        for m in range(s):
            pltpu.make_async_copy(
                turned.at[:, jnp.bitwise_xor(me, m)], outs[m], out_sem.at[m]
            ).wait()
    for store in stores:
        store.wait()


def prep(plan, tokens, chunk, split):
    bf16 = jnp.bfloat16
    if split:
        shapes = [jax.ShapeDtypeStruct((plan.rows, plan.own, plan.width), bf16)] * plan.seq
        shape = (plan.out_rows, plan.seq, plan.own, plan.width)
        shapes += [jax.ShapeDtypeStruct(shape, bf16)] * plan.ch
    else:
        shape = (plan.seq, plan.rows, plan.own, plan.width)
        shapes = [jax.ShapeDtypeStruct(shape, bf16)]
    out = pl.pallas_call(
        functools.partial(prep_kernel, plan, chunk, split),
        out_shape=shapes,
        in_specs=[ANY],
        out_specs=[ANY] * len(shapes),
        scratch_shapes=[
            pltpu.VMEM((plan.rows, plan.width, plan.chunk), bf16),
            pltpu.VMEM((plan.rows, plan.seq, plan.own, plan.width), bf16),
            pltpu.SemaphoreType.DMA((plan.rows,)),
            pltpu.SemaphoreType.DMA((max(plan.seq, plan.rows),)),
            pltpu.SemaphoreType.DMA((plan.ch,)),
        ],
        cost_estimate=pl.CostEstimate(
            flops=0,
            bytes_accessed=6 * plan.rows * plan.chunk * plan.width,
            transcendentals=0,
        ),
        compiler_params=pltpu.CompilerParams(vmem_limit_bytes=GRANT),
        name="prep",
    )(tokens)
    if split:
        shape = (plan.out_rows, plan.chunk, plan.width)
        return out[: plan.seq], [share.reshape(shape) for share in out[plan.seq :]]
    return out[0], [own_rows(plan, out[0], n) for n in range(plan.ch)]


def own_rows(plan, block, mask):
    start = jnp.bitwise_xor(lax.axis_index("ch"), mask) * plan.out_rows
    part = lax.dynamic_slice_in_dim(block, start, plan.out_rows, axis=1)
    return part.transpose(1, 0, 2, 3).reshape(plan.out_rows, plan.chunk, plan.width)


def sections_kernel(plan, count, full, *refs):
    near, far, own = plan.near, plan.seq // plan.near, plan.own
    pieces, gathered, left = refs[:count], refs[count : count + near], refs[count + near]
    parts = 1 + plan.half * plan.ch * (2 if full else 1)
    outs = refs[count + near + 1 : count + near + 1 + parts]
    x, right, twiddle, first, mixed, out = refs[count + near + 1 + parts : -5]
    sem_x, sem_r, sem_t, sem_o, sem_l = refs[-5:]
    me, y = lax.axis_index("seq"), lax.axis_index("ch")
    if count == 1:
        copies = [pltpu.make_async_copy(pieces[0], x, sem_x.at[0])]
    else:
        copies = [
            pltpu.make_async_copy(
                pieces[m], x.at[pl.ds(jnp.bitwise_xor(me, m) * plan.rows, plan.rows)], sem_x.at[m]
            )
            for m in range(count)
        ]
    for m in range(near):
        for n in range(far):
            who = jnp.bitwise_xor(me, n * near + m)
            at = pl.ds(pl.multiple_of(who * plan.right_rows, plan.right_rows), plan.right_rows)
            source = gathered[m].at[n]
            copies.append(
                pltpu.make_async_copy(
                    source.at[pl.ds(0, plan.right_rows)], right.at[at], sem_r.at[m * far + n]
                )
            )
            copies.append(
                pltpu.make_async_copy(
                    source.at[pl.ds(plan.right_rows, plan.rows)],
                    twiddle.at[who],
                    sem_t.at[m * far + n],
                )
            )
    kt = pl.program_id(0)

    @pl.when(kt == 0)
    def _():
        for copy in copies:
            copy.start()
        for copy in copies:
            copy.wait()

    ks = pl.ds(pl.multiple_of(kt * LANES, LANES), LANES)

    def section_one(t, carry):
        rows = x[pl.ds(t * STEP, STEP)].reshape(STEP * own, plan.width)
        value = jnp.dot(rows, right[:, ks], preferred_element_type=jnp.float32)
        value = value.reshape(STEP, own, LANES)
        group = STEP // plan.rows
        factor = twiddle[pl.ds(t * group, group), :, ks].astype(jnp.float32)
        value = value * factor.reshape(STEP, LANES)[:, None, :]
        at = pl.ds(pl.multiple_of(t * STEP, STEP), STEP)
        first[:, at, :] = jnp.swapaxes(value, 0, 1).astype(jnp.bfloat16)
        return carry

    lax.fori_loop(0, plan.all_rows // STEP, section_one, 0)
    for q in range(own):
        mixed[q] = jnp.dot(left[...], first[q], preferred_element_type=jnp.float32)

    def turn(t, carry):
        at = pl.ds(pl.multiple_of(t * STEP, STEP), STEP)
        value = jnp.swapaxes(mixed[:, at, :], 0, 1)
        out[pl.ds(t * STEP, STEP), :, ks] = value.astype(jnp.bfloat16)
        return carry

    lax.fori_loop(0, plan.all_rows // STEP, turn, 0)

    @pl.when(kt == plan.width // LANES - 1)
    def _():
        half, ways, rows = plan.half, plan.half * plan.ch, plan.out_rows
        stores = []
        low = 0 if full else half
        for m in range((plan.seq - low) * plan.ch):
            row = jnp.bitwise_xor(me, low + m // plan.ch) * plan.rows
            row = row + jnp.bitwise_xor(y, m % plan.ch) * rows
            at = pl.ds(row + full, rows - full)
            stores.append(pltpu.make_async_copy(out.at[at], outs[1 + m], sem_o.at[m]))
        for m in range(2 * ways if full else ways):
            row = m * rows if full else (me // half) * (half * plan.rows) + m * rows
            at = pl.ds(row, full if full else rows)
            stores.append(pltpu.make_async_copy(out.at[at], outs[0].at[m], sem_l.at[m]))
        for store in stores:
            store.start()
        for store in stores:
            store.wait()


def sections(plan, pieces, gathered, left, full):
    s, own, width, bf16 = plan.seq, plan.own, plan.width, jnp.bfloat16
    flops = 2 * plan.all_rows * own * width * (width + plan.all_rows)
    ways = plan.half * plan.ch
    count = 2 * ways if full else ways
    shapes = [jax.ShapeDtypeStruct((count, full if full else plan.out_rows, own, width), bf16)]
    shapes += [jax.ShapeDtypeStruct((plan.out_rows - full, own, width), bf16)] * count
    return pl.pallas_call(
        functools.partial(sections_kernel, plan, len(pieces), full),
        out_shape=shapes,
        grid=(width // LANES,),
        in_specs=[ANY] * (len(pieces) + len(gathered)) + [VMEM],
        out_specs=[ANY] * len(shapes),
        scratch_shapes=[
            pltpu.VMEM((plan.all_rows, own, width), bf16),
            pltpu.VMEM((s * plan.right_rows, width), bf16),
            pltpu.VMEM((s, plan.rows, width), bf16),
            pltpu.VMEM((own, plan.all_rows, LANES), bf16),
            pltpu.VMEM((own, plan.all_rows, LANES), jnp.float32),
            pltpu.VMEM((plan.all_rows, own, width), bf16),
            pltpu.SemaphoreType.DMA((s,)),
            pltpu.SemaphoreType.DMA((s,)),
            pltpu.SemaphoreType.DMA((s,)),
            pltpu.SemaphoreType.DMA((2 * ways,)),
            pltpu.SemaphoreType.DMA((2 * ways,)),
        ],
        cost_estimate=pl.CostEstimate(
            flops=flops,
            bytes_accessed=4 * plan.all_rows * own * width + 2 * width * width,
            transcendentals=0,
        ),
        compiler_params=pltpu.CompilerParams(vmem_limit_bytes=GRANT),
        name="sections",
    )(*pieces, *gathered, left)


def load_piece(plan, piece, mixed, sem):
    for r in range(piece.shape[1]):
        for m in range(plan.seq * plan.ch):
            row = (m % plan.ch) * plan.chunk + (m // plan.ch) * plan.own
            pltpu.make_async_copy(
                piece.at[m, r], mixed.at[r, pl.ds(row, plan.own)], sem.at[r]
            ).start()


def load_halves(plan, block, pieces, mixed, sem):
    me, y = lax.axis_index("seq"), lax.axis_index("ch")
    half, own = plan.half, plan.own
    for r in range(block.shape[1]):
        for m in range(half * plan.ch):
            row = (m % plan.ch) * plan.chunk + ((me // half) * half + m // plan.ch) * own
            pltpu.make_async_copy(
                block.at[m, r], mixed.at[r, pl.ds(pl.multiple_of(row, own), own)], sem.at[r]
            ).start()
            who = jnp.bitwise_xor(me, half + m // plan.ch)
            row = jnp.bitwise_xor(y, m % plan.ch) * plan.chunk + who * own
            pltpu.make_async_copy(
                pieces[m].at[r], mixed.at[r, pl.ds(pl.multiple_of(row, own), own)], sem.at[r]
            ).start()


def load_pieces(plan, pieces, mixed, sem):
    me, y = lax.axis_index("seq"), lax.axis_index("ch")
    for r in range(pieces[0].shape[0]):
        for m, piece in enumerate(pieces):
            row = jnp.bitwise_xor(y, m % plan.ch) * plan.chunk
            row = row + jnp.bitwise_xor(me, m // plan.ch) * plan.own
            at = pl.ds(pl.multiple_of(row, plan.own), plan.own)
            pltpu.make_async_copy(piece.at[r], mixed.at[r, at], sem.at[r]).start()


def load_shares(plan, shares, inputs, sem):
    y = lax.axis_index("ch")
    for r in range(plan.out_rows):
        for n in range(plan.ch):
            at = pl.ds(jnp.bitwise_xor(y, n) * plan.chunk, plan.chunk)
            pltpu.make_async_copy(shares[n].at[r], inputs.at[r, at], sem.at[r]).start()


def wait_row(buffer, sem, r):
    pltpu.make_async_copy(buffer.at[r], buffer.at[r], sem.at[r]).wait()


def column(plan, chunk, j):
    row = j * plan.mix
    return (row // plan.chunk) * plan.local + chunk * plan.chunk + row % plan.chunk


def silu(value):
    return value / (1.0 + jnp.exp(-value))


def turn_dot(value, weight):
    return lax.dot_general(
        value, weight, (((0,), (0,)), ((), ())), preferred_element_type=jnp.float32
    )


def gate_kernel(plan, *refs):
    c = plan.ch
    count = 1 + plan.half * c
    block, pieces, refs = refs[0], refs[1:count], refs[count:]
    shares, later = refs[:c], refs[c : 2 * c]
    gain, weight, out, gates, totals = refs[2 * c : 5 + 2 * c]
    mixed, inputs, after, sem_m, sem_i, sem_a = refs[5 + 2 * c :]
    i = pl.program_id(0)

    @pl.when(i == 0)
    def _():
        load_shares(plan, later, after, sem_a)
        load_shares(plan, shares, inputs, sem_i)
        load_halves(plan, block, pieces, mixed, sem_m)

    wait_row(after, sem_a, i)
    wait_row(inputs, sem_i, i)
    wait_row(mixed, sem_m, i)

    def tile(kt, carry):
        ks = pl.ds(pl.multiple_of(kt * LANES, LANES), LANES)
        total = jnp.zeros((1, LANES), jnp.float32)
        for j in range(plan.chunk * c // plan.mix):
            rs = pl.ds(j * plan.mix, plan.mix)
            gates[0, rs, ks] = silu(after[i, rs, ks].astype(jnp.float32)).astype(jnp.bfloat16)
            value = mixed[i, rs, ks].astype(jnp.float32)
            value = value * silu(inputs[i, rs, ks].astype(jnp.float32))
            value = value.astype(jnp.bfloat16).astype(jnp.float32)
            total = total + jnp.sum(value * value, axis=0, keepdims=True)
            col = column(plan, 0, j)
            value = (value * gain[pl.ds(col, plan.mix), :]).astype(jnp.bfloat16)
            out[ks, rs] = turn_dot(value, weight[col // plan.mix]).astype(jnp.bfloat16)
        totals[0, :, ks] = jnp.broadcast_to(total, (8, LANES))
        return carry

    lax.fori_loop(0, plan.width // LANES, tile, 0)


def final_kernel(plan, count, base, rows, *refs):
    pieces, gates, held, sums, gains, weights = refs[:count], *refs[count : count + 5]
    result = refs[-13]
    mixed, inputs, left, out, before, gain, weight = refs[-12:-5]
    sem_m, sem_i, sem_h, sem_o, sem_c = refs[-5:]
    c, width = plan.ch, plan.width
    blocks = plan.chunk * c // plan.mix
    constants = [
        pltpu.make_async_copy(sums.at[pl.ds(base, rows)], before, sem_c.at[0]),
        pltpu.make_async_copy(gains, gain, sem_c.at[1]),
    ]
    for j in range(blocks):
        block = weights.at[column(plan, 1, j) // plan.mix]
        constants.append(pltpu.make_async_copy(block, weight.at[j], sem_c.at[2 + j]))
    for constant in constants:
        constant.start()
    for r in range(rows):
        pltpu.make_async_copy(gates.at[base + r], inputs.at[r], sem_i.at[r]).start()
        at = pl.ds((base + r) * width, width)
        pltpu.make_async_copy(held.at[at], left.at[r], sem_h.at[r]).start()
    if count == 1:
        load_piece(plan, pieces[0], mixed, sem_m)
    else:
        load_pieces(plan, pieces, mixed, sem_m)
    tiles = width // LANES
    for constant in constants:
        constant.wait()
    for r in range(rows):
        wait_row(inputs, sem_i, r)
        wait_row(left, sem_h, r)
        wait_row(mixed, sem_m, r)

        def tile(kt, carry):
            ks = pl.ds(pl.multiple_of(kt * LANES, LANES), LANES)
            total = before[r, pl.ds(0, 1), ks]
            parts = []
            for j in range(plan.chunk * c // plan.mix):
                rs = pl.ds(j * plan.mix, plan.mix)
                value = mixed[r, rs, ks].astype(jnp.float32)
                value = value * inputs[r, rs, ks].astype(jnp.float32)
                total = total + jnp.sum(value * value, axis=0, keepdims=True)
                col = column(plan, 1, j)
                value = (value * gain[rs, :]).astype(jnp.bfloat16)
                parts.append((col, turn_dot(value, weight[j])))
            inverse = lax.rsqrt(total * (1.0 / plan.channels) + 1e-05)
            scale = jnp.broadcast_to(inverse, (128, LANES)).T
            for col, part in parts:
                for q in range(plan.mix // 128):
                    value = part[:, q * 128 : (q + 1) * 128] * scale
                    out[r, ks, pl.ds(col + q * 128, 128)] = value.astype(jnp.bfloat16)
            for j in range(plan.chunk * c // 128):
                value = left[r, ks, pl.ds(j * 128, 128)].astype(jnp.float32) * scale
                col = (j * 128 // plan.chunk) * plan.local + j * 128 % plan.chunk
                out[r, ks, pl.ds(col, 128)] = value.astype(jnp.bfloat16)
            at = pl.ds(pl.multiple_of((base + r) * width + kt * LANES, LANES), LANES)
            pltpu.make_async_copy(out.at[r, ks], result.at[at], sem_o.at[r]).start()
            return carry

        lax.fori_loop(0, tiles, tile, 0)
    for r in range(rows):
        at = pl.ds((base + r) * width, width)
        pltpu.make_async_copy(out.at[r], result.at[at], sem_o.at[r]).wait()


def gate(plan, pieces, shares, later, gain, weight):
    size, part = plan.out_rows * plan.width, plan.chunk * plan.ch
    shape, bf16 = (plan.out_rows, part, plan.width), jnp.bfloat16
    sem = pltpu.SemaphoreType.DMA((plan.out_rows,))
    return pl.pallas_call(
        functools.partial(gate_kernel, plan),
        out_shape=[
            jax.ShapeDtypeStruct((size, part), bf16),
            jax.ShapeDtypeStruct(shape, bf16),
            jax.ShapeDtypeStruct((plan.out_rows, 8, plan.width), jnp.float32),
        ],
        grid=(plan.out_rows,),
        in_specs=[ANY] * (len(pieces) + 2 * plan.ch) + [VMEM, VMEM],
        out_specs=[
            pl.BlockSpec((plan.width, part), lambda i: (i, 0)),
            pl.BlockSpec((1, part, plan.width), lambda i: (i, 0, 0)),
            pl.BlockSpec((1, 8, plan.width), lambda i: (i, 0, 0)),
        ],
        scratch_shapes=[pltpu.VMEM(shape, bf16)] * 3 + [sem] * 3,
        cost_estimate=pl.CostEstimate(
            flops=2 * size * part * plan.mix,
            bytes_accessed=10 * size * part,
            transcendentals=2 * size * part,
        ),
        compiler_params=pltpu.CompilerParams(vmem_limit_bytes=GRANT),
        name="gate",
    )(*pieces, *shares, *later, gain, weight)


def final(plan, pieces, gates, held, before, gain, weight, base, rows, result=None):
    size, part = rows * plan.width, plan.chunk * plan.ch
    shape, bf16 = (rows, part, plan.width), jnp.bfloat16
    sem = pltpu.SemaphoreType.DMA((rows,))
    args = [*pieces, gates, held, before, gain, weight]
    aliases = {}
    if result is not None:
        aliases[len(args)] = 0
        args.append(result)
    return pl.pallas_call(
        functools.partial(final_kernel, plan, len(pieces), base, rows),
        out_shape=jax.ShapeDtypeStruct((plan.out_rows * plan.width, plan.channels), bf16),
        in_specs=[ANY] * len(args),
        out_specs=ANY,
        input_output_aliases=aliases,
        scratch_shapes=[
            pltpu.VMEM(shape, bf16),
            pltpu.VMEM(shape, bf16),
            pltpu.VMEM((rows, plan.width, part), bf16),
            pltpu.VMEM((rows, plan.width, plan.channels), bf16),
            pltpu.VMEM((rows, 8, plan.width), jnp.float32),
            pltpu.VMEM((part, LANES), jnp.float32),
            pltpu.VMEM((part // plan.mix, plan.mix, plan.mix), bf16),
        ]
        + [sem] * 4
        + [pltpu.SemaphoreType.DMA((2 + part // plan.mix,))],
        cost_estimate=pl.CostEstimate(
            flops=2 * size * part * plan.mix,
            bytes_accessed=10 * size * part,
            transcendentals=0,
        ),
        compiler_params=pltpu.CompilerParams(vmem_limit_bytes=GRANT),
        name="final",
    )(*args)


def swap(value, mask, axis):
    count = lax.axis_size(axis)
    return lax.ppermute(value, axis, [(i, i ^ mask) for i in range(count)])


def exchange(value, axes):
    return lax.all_to_all(value, axes, split_axis=0, concat_axis=0, tiled=True)


def chunked_body(plan, tokens, right_block, twiddle, left_block, gain, mix_weight):
    s, c, near, own = plan.seq, plan.ch, plan.near, plan.own
    pad = plan.gather_rows - right_block.shape[0] - twiddle.shape[0]
    zeros = jnp.zeros((pad, plan.width), jnp.bfloat16)
    held = jnp.concatenate([right_block, twiddle, zeros], axis=0)[None]
    later = gain.reshape(c, CHUNKS, plan.chunk)[:, 1].reshape(c * plan.chunk, 1)
    later = jnp.broadcast_to(later, (c * plan.chunk, LANES))
    gain = jnp.broadcast_to(gain[:, None], (plan.channels, LANES))
    gain, later = lax.optimization_barrier((gain, later))
    column = [held]
    for n in range(1, s // near):
        column.append(swap(held, n * near, "seq"))
    column = jnp.concatenate(column, axis=0)
    gathered = [column]
    for m in range(1, near):
        gathered.append(swap(column, m, "seq"))
    arrived, shares = [], []
    for k in range(CHUNKS):
        pieces, share = prep(plan, tokens, k, k == 1)
        if k == 0:
            block = exchange(pieces, "seq")
            arrived.append([block.reshape(plan.all_rows, own, plan.width)])
        else:
            arrived.append([pieces[0]] + [None] * (s - 1))
            for m in reversed(range(1, s)):
                arrived[k][m] = swap(pieces[m], m, "seq")
        shares.append([share[0]])
        for n in range(1, c):
            shares[k].append(swap(share[n], n, "ch"))
    half, ways = plan.half, plan.half * c
    groups = [[h * ways + i for i in range(ways)] for h in range(2)]
    first = plan.out_rows - LAST
    landed = []
    for k in range(CHUNKS):
        block, *pieces = sections(plan, arrived[k], gathered, left_block, k * first)
        low = 0 if k else half
        if k:
            block = exchange(block, ("seq", "ch"))
        else:
            block = lax.all_to_all(block, ("seq", "ch"), 0, 0, axis_index_groups=groups, tiled=True)
        landed.append([block])
        for m in range(low, s):
            for n in range(c):
                piece = pieces[(m - low) * c + n]
                if m or n:
                    piece = cross(piece, m, n, s, c)
                landed[k].append(piece)
    held, gates, before = gate(plan, landed[0], *shares, gain, mix_weight)
    rest = (gates, held, before, later, mix_weight)
    result = final(plan, landed[1][:1], *rest, 0, first)
    return final(plan, landed[1][1:], *rest, first, LAST, result)


def cross(value, seq_mask, ch_mask, s, c):
    pairs = [(i * c + j, (i ^ seq_mask) * c + (j ^ ch_mask)) for i in range(s) for j in range(c)]
    return lax.ppermute(value, ("seq", "ch"), pairs)


def plain_body(tokens, right_block, twiddle, left_block, gain, mix_weight):
    row_width = right_block.shape[1]
    row_count = tokens.shape[0] // row_width
    local_width = tokens.shape[1]
    inputs = tokens.reshape(row_count, row_width, local_width)
    whole_right = lax.all_gather(right_block, "seq", axis=0, tiled=True)
    first_section = jnp.einsum(
        "abc,bk->akc", inputs, whole_right, preferred_element_type=jnp.float32
    )
    spread = (first_section * twiddle.astype(jnp.float32)[:, :, None]).astype(jnp.bfloat16)
    mixed_rows = jnp.einsum(
        "ij,jbc->ibc",
        left_block,
        lax.all_to_all(spread, "seq", split_axis=1, concat_axis=0, tiled=True),
        preferred_element_type=jnp.float32,
    ).astype(jnp.bfloat16)
    sequence_mixed = lax.all_to_all(mixed_rows, "seq", split_axis=0, concat_axis=1, tiled=True)
    gated = (sequence_mixed.astype(jnp.float32) * jax.nn.silu(inputs.astype(jnp.float32))).astype(
        jnp.bfloat16
    )
    ch_count = lax.axis_size("ch")
    pieces = gated.reshape(ch_count, row_count * row_width // ch_count, local_width)
    shard_piece = lax.all_to_all(pieces, "ch", split_axis=0, concat_axis=2, tiled=True)
    values = shard_piece.astype(jnp.float32)
    inverse_rms = lax.rsqrt(jnp.mean(values * values, axis=-1, keepdims=True) + 1e-05)
    normed = (values * inverse_rms * gain).astype(jnp.bfloat16)
    block_count = mix_weight.shape[0]
    block_width = mix_weight.shape[1]
    normed = normed.reshape(shard_piece.shape[0], shard_piece.shape[1], block_count, block_width)
    result = jnp.einsum("otki,kij->otkj", normed, mix_weight, preferred_element_type=jnp.float32)
    mixed_out = result.astype(jnp.bfloat16).reshape(shard_piece.shape)
    return mixed_out.reshape(mixed_out.shape[1], mixed_out.shape[2])


def body(tokens, right_block, twiddle, left_block, gain, mix_weight):
    plan = Plan(tokens, right_block, twiddle, left_block, mix_weight)
    if plan.fits():
        return chunked_body(plan, tokens, right_block, twiddle, left_block, gain, mix_weight)
    return plain_body(tokens, right_block, twiddle, left_block, gain, mix_weight)


def solution(mesh):
    in_specs = (P("seq", "ch"), P("seq", None), P("seq", None), P(), P(), P())
    out_specs = P(("seq", "ch"), None)
    return jax.shard_map(body, mesh=mesh, in_specs=in_specs, out_specs=out_specs, check_vma=False)
```
